256 devices in a mesh: chan: 32 (over y_lo, z, core), win: 8 (over y_hi, x).
Axes of the slice: x: 4, y: 4 (y_hi: 2, y_lo: 2; y = y_hi * 2 + y_lo), z: 8, core: 2. Of those that a mesh axis runs over, the one named last changes fastest.
Arguments:
- traces: bfloat16 [96, 2048, 4096], P('win', 'chan'), may hold values from -6 to 6
- quality: int32 [2048], P('chan'), may hold values 0 or 1
- fold_block: int32 [2048, 1], replicated, may hold values from 0 to 31; in each aligned block of 64 rows (0 to 63, 64 to 127, ...) at most 8 rows name the same one
- fold_offset: int32 [2048], replicated, may hold values from 0 to 63
Outputs:
- neighbour_lags: float32 [2048, 64, 256], P(('chan', 'win'))
- fold_lags: float32 [2048, 256], P(('chan', 'win'))
The draws below stay inside these ranges and needn't reach their ends.
Inputs may be any that keep to these rules, and one draw needn't show every extreme that they name: `fold_block`: within each aligned block of 64 channels no block number appears more than 8 times.
All inputs are finite; a program needn't handle non-finite values. No bound on the sum of `quality` on one device may be relied on, other than what follows from the above.
Results may differ from the reference program's by a relative error of at most 0.0052.
Values may be sent and summed in bfloat16 or wider, within the bound.
A program may use at most 128 MiB of HBM per device.

```python
import math
import jax
import jax.numpy as jnp
import numpy as np
from jax import lax

L = 4096
F = 256
BAND_LO = 32
NLAG = 256
REACH = 64
CAP = 8
CH_DEV = 64
CHANNELS = 2048
WINDOWS = 96
N_CHAN = 32


def plant(array, rng, least, high):
    longest = array.shape.index(max(array.shape))
    spots = []
    for shift in (0, 1):
        where = [jax.random.randint(jax.random.fold_in(rng, axis), (), 0, length) for axis, length in enumerate(array.shape)]
        where[longest] = (where[longest] + shift) % array.shape[longest]
        spots.append(tuple(where))
    return array.at[spots[0]].set(least).at[spots[1]].set(high)


def block_levels(stream_key, dims, pieces, least, high):
    factor_of = 1.0
    for position, parts in pieces:
        heights = jax.random.uniform(jax.random.fold_in(jax.random.fold_in(stream_key, 6), position), (parts,), jnp.float32, least / len(pieces), high / len(pieces))
        factor_of = factor_of * jnp.repeat(jnp.exp(heights), dims[position] // parts).reshape((-1,) + (1,) * (len(dims) - 1 - position))
    return factor_of


def routed_block(rng, own, number, rows, number_of, top, reach, skew):
    ranking = jax.random.permutation(rng, number_of)
    crowded, ordinary = portions_of(number_of, rows * top, reach, skew, True), portions_of(number_of, rows * top, reach, skew, False)
    places = jnp.arange(number_of)

    def named(sizes, offset_by):
        used = int((sizes > 0).sum())
        fixed = max(1, used // 4)
        moved = fixed + (places - fixed + offset_by * (used - fixed)) % max(1, number_of - fixed)
        return jnp.zeros((number_of,), jnp.int32).at[ranking[jnp.where(places < fixed, places, moved)]].set(jnp.asarray(sizes, jnp.int32))

    sizes = jnp.where(number % 4 == 0, named(crowded, number // 4), named(ordinary, number - number // 4 - 1))
    mixed = jax.random.permutation(jax.random.fold_in(own, 3), number_of)
    donor, receiver = mixed[0:number_of // 2 * 2:2], mixed[1:number_of // 2 * 2:2]
    room = jnp.minimum(sizes[donor] - 1, reach - sizes[receiver]) // 2
    room = jnp.where((donor == ranking[0]) | (receiver == ranking[0]) | (sizes[receiver] == 0), 0, jnp.maximum(room, 0))
    moved = jax.random.randint(jax.random.fold_in(own, 4), (number_of // 2,), 0, 1 << 20) % (room + 1)
    sizes = sizes.at[donor].add(-moved).at[receiver].add(moved)
    labels = jnp.searchsorted(jnp.cumsum(sizes), jnp.arange(rows * top), side="right").astype(jnp.int32)
    listing = labels.reshape(top, rows).T
    listing = listing[jax.random.permutation(jax.random.fold_in(own, 1), rows)]
    offset_by = jax.random.randint(jax.random.fold_in(own, 2), (rows, 1), 0, top)
    return jnp.take_along_axis(listing, (jnp.arange(top)[None, :] + offset_by) % top, axis=1)


def portions_of(count, total, bound, skew, full):
    weights = [(1 << 20) // math.isqrt(grade ** skew) + 1 for grade in range(1, count + 1)]
    largest = bound if full else min(bound, max(-(-total // count), total * weights[0] // sum(weights)))
    least = 1 if total - largest >= count - 1 else 0
    holding, rest = [largest] + [least] * (count - 1), total - largest - least * (count - 1)
    while rest > 0:
        free = [i for i in range(1, count) if holding[i] < largest] or [i for i in range(1, count) if holding[i] < bound]
        pool, remaining = sum([weights[i] for i in free]), rest
        for i in free:
            extra = min(bound - holding[i], max(1, remaining * weights[i] // pool), rest)
            holding[i] = holding[i] + extra
            rest = rest - extra
    return np.array(holding)


def bell_draw(key, extent, deviation, limit, split=(), kind=jnp.bfloat16):
    gain = block_levels(key, extent, split, -0.22, 0.18) if split else 1.0
    entries = jax.random.normal(key, extent, jnp.float32) * deviation * gain
    return jnp.minimum(jnp.maximum(entries, -limit), limit).astype(kind)


def setup_inputs(seed: int = 0) -> dict:
    key_of = jax.random.split(jax.random.key(seed), 5)
    traces = bell_draw(key_of[0], (WINDOWS, CHANNELS, L), 1.0, 6.0, ((0, 8), (1, 32)))
    quality = plant((jax.random.randint(key_of[1], (CHANNELS,), 0, 8) < 7).astype(jnp.int32), jax.random.fold_in(key_of[1], 1), 0, 1)
    fold_block_keys = jax.random.split(jax.random.fold_in(key_of[2], 1), CHANNELS // CH_DEV)
    fold_block_turns = jax.random.permutation(jax.random.fold_in(key_of[2], 3), CHANNELS // CH_DEV)
    fold_block = jax.vmap(lambda own, number: routed_block(jax.random.fold_in(key_of[2], 2), own, number, CH_DEV, N_CHAN, 1, CAP, 1))(fold_block_keys, fold_block_turns).reshape((CHANNELS, 1))
    fold_offset = plant(jax.random.randint(key_of[3], (CHANNELS,), 0, CH_DEV), jax.random.fold_in(key_of[3], 1), 0, CH_DEV - 1).astype(jnp.int32)
    return dict(traces=traces, quality=quality, fold_block=fold_block, fold_offset=fold_offset)


smooth_reach = 4

def forward_table(length, bin_count, lowest):
    samples = jnp.arange(length, dtype=jnp.int32)[:, None]
    frequency = (jnp.arange(bin_count, dtype=jnp.int32) + lowest)[None, :]
    angles = (samples * frequency % length).astype(jnp.float32) * (2.0 * math.pi / length)
    return jnp.concatenate([jnp.cos(angles), -jnp.sin(angles)], axis=1).astype(jnp.bfloat16)

def inverse_table(bin_count, lowest, lag_count):
    shifts = jnp.arange(lag_count, dtype=jnp.int32)[None, :] + lag_count // 2
    frequency = (jnp.arange(bin_count, dtype=jnp.int32) + lowest)[:, None]
    angles = (frequency * shifts % lag_count).astype(jnp.float32) * (2.0 * math.pi / lag_count)
    return jnp.concatenate([jnp.cos(angles), -jnp.sin(angles)], axis=0)

def whiten(spectra, keep_mask):
    bin_count = spectra.shape[-1] // 2
    real_part = spectra[..., :bin_count]
    imag_part = spectra[..., bin_count:]
    energy = real_part * real_part + imag_part * imag_part
    padded = jnp.pad(energy, ((0, 0), (0, 0), (smooth_reach, smooth_reach)))
    smooth = sum([padded[..., offset:offset + bin_count] for offset in range(2 * smooth_reach + 1)]) / (2.0 * smooth_reach + 1.0)
    water_level = lax.optimization_barrier(jnp.mean(energy, axis=-1, keepdims=True))
    scaling = lax.rsqrt(smooth + 0.1 * water_level + 1e-06) * keep_mask[None, :, None]
    return jnp.concatenate([real_part * scaling, imag_part * scaling], axis=-1).astype(jnp.bfloat16)

def cross_spectrum(left_block, right_block):
    half_width = left_block.shape[-1] // 2
    left_real = left_block[..., :half_width].astype(jnp.float32)
    left_imag = left_block[..., half_width:].astype(jnp.float32)
    right_real = right_block[..., :half_width].astype(jnp.float32)
    right_imag = right_block[..., half_width:].astype(jnp.float32)
    real_part = lax.optimization_barrier(jnp.sum(left_real * right_real + left_imag * right_imag, axis=0))
    imag_part = lax.optimization_barrier(jnp.sum(left_imag * right_real - left_real * right_imag, axis=0))
    return jnp.concatenate([real_part, imag_part], axis=-1)

def reference(traces, quality, fold_block, fold_offset):
    forward = forward_table(L, F, BAND_LO)
    keep_mask = quality.astype(jnp.float32)

    def one_window(window_traces):
        spectra = jnp.dot(window_traces, forward, preferred_element_type=jnp.float32)
        return whiten(spectra[None], keep_mask)[0]
    whitened = lax.map(one_window, traces)
    padded = jnp.pad(whitened, ((0, 0), (0, REACH), (0, 0)))

    def one_offset(offset):
        shifted = lax.dynamic_slice_in_dim(padded, offset, CHANNELS, axis=1)
        return cross_spectrum(whitened, shifted)
    offsets = jnp.arange(1, REACH + 1, dtype=jnp.int32)
    neighbour_terms = lax.map(one_offset, offsets)
    partner_index = (fold_block[:, 0] * CH_DEV + fold_offset).astype(jnp.int32)
    partner_terms = cross_spectrum(whitened, jnp.take(whitened, partner_index, axis=1))
    stacks = jnp.concatenate([jnp.transpose(neighbour_terms, (1, 0, 2)), partner_terms[:, None, :]], axis=1)
    inverse = inverse_table(F, BAND_LO, NLAG)
    factor = 1.0 / math.sqrt(F * WINDOWS)
    lagged = jnp.einsum('cpf,fl->cpl', stacks, inverse, precision=lax.Precision.HIGHEST) * factor
    return (lagged[:, :REACH, :], lagged[:, REACH, :])
```

```python
import math

import jax
import jax.numpy as jnp
import numpy as np
from jax import lax
from jax.experimental import pallas as pl
from jax.experimental.pallas import tpu as pltpu
from jax.sharding import PartitionSpec as P

F = 256
BAND_LO = 32
NLAG = 256
REACH = 64
L = 4096
CH_DEV = 64
CHANNELS = 2048
WINDOWS = 96
N_CHAN = 32
N_WIN = 8
WIN_DEV = WINDOWS // N_WIN
ROWS = CHANNELS // (N_CHAN * N_WIN)
SMOOTH = 4
STEP = 128
GROUP = 4
SENT_ROWS = 12


def phase_tables(samples, stride):
    frequency = np.arange(F, dtype=np.int64)[:, None] + BAND_LO
    steps = np.arange(samples, dtype=np.int64)[None, :] * stride
    angles = (frequency * steps % L).astype(np.float64) * (2.0 * math.pi / L)
    return np.cos(angles).astype(np.float32), np.sin(angles).astype(np.float32)


def inverse_table():
    shifts = np.arange(NLAG, dtype=np.int64)[None, :] + NLAG // 2
    frequency = np.arange(F, dtype=np.int64)[:, None] + BAND_LO
    angles = (frequency * shifts % NLAG).astype(np.float64) * (2.0 * math.pi / NLAG)
    return np.cos(angles).astype(np.float32), (-np.sin(angles)).astype(np.float32)


def whiten_kernel(x_ref, q_ref, fc_ref, fs_ref, cc_ref, cs_ref, o_ref, table, energy):
    @pl.when(pl.program_id(0) == 0)
    def _():
        fine_cos, fine_sin = fc_ref[...], fs_ref[...]
        for block in range(L // STEP):
            cos_b = cc_ref[:, block : block + 1]
            sin_b = cs_ref[:, block : block + 1]
            lanes = slice(block * STEP, (block + 1) * STEP)
            table[0:F, lanes] = (fine_cos * cos_b - fine_sin * sin_b).astype(jnp.bfloat16)
            table[F : 2 * F, lanes] = (-fine_sin * cos_b - fine_cos * sin_b).astype(jnp.bfloat16)
        energy[0:8, :] = jnp.zeros((8, GROUP * CH_DEV), jnp.float32)
        energy[8 + F : 16 + F, :] = jnp.zeros((8, GROUP * CH_DEV), jnp.float32)

    spectra = lax.dot_general(
        table[...], x_ref[...], (((1,), (1,)), ((), ())), preferred_element_type=jnp.float32
    )
    real_part, imag_part = spectra[0:F], spectra[F : 2 * F]
    power = real_part * real_part + imag_part * imag_part
    energy[8 : 8 + F, :] = power
    smooth = power
    for shift in range(1, SMOOTH + 1):
        smooth = smooth + (energy[8 - shift : 8 - shift + F, :] + energy[8 + shift : 8 + shift + F, :])
    water = jnp.sum(power, axis=0, keepdims=True) * (1.0 / F)
    scaling = lax.rsqrt(smooth * (1.0 / (2 * SMOOTH + 1)) + 0.1 * water + 1e-06) * q_ref[...]
    real_part = real_part * scaling
    imag_part = imag_part * scaling
    low = lax.broadcasted_iota(jnp.int32, (F, 128), 1) < CH_DEV
    for pair in range(GROUP // 2):
        re = real_part[:, pair * 128 : pair * 128 + 128]
        im = imag_part[:, pair * 128 : pair * 128 + 128]
        first = jnp.where(low, re, pltpu.roll(im, CH_DEV, 1))
        second = jnp.where(low, pltpu.roll(re, CH_DEV, 1), im)
        o_ref[:, pair * 256 : pair * 256 + 128] = first.astype(jnp.bfloat16)
        o_ref[:, pair * 256 + 128 : pair * 256 + 256] = second.astype(jnp.bfloat16)


def whiten(traces, quality):
    fine = phase_tables(STEP, 1)
    coarse = phase_tables(L // STEP, STEP)
    lanes = GROUP * CH_DEV
    q = jnp.tile(quality.astype(jnp.float32), GROUP)[None, :]
    whole = lambda shape: pl.BlockSpec(shape, lambda i: (0, 0))
    return pl.pallas_call(
        whiten_kernel,
        grid=(WIN_DEV // GROUP,),
        out_shape=jax.ShapeDtypeStruct((F, WIN_DEV * 128), jnp.bfloat16),
        in_specs=[
            pl.BlockSpec((lanes, L), lambda i: (i, 0)),
            whole((1, lanes)),
            whole((F, STEP)),
            whole((F, STEP)),
            whole((F, L // STEP)),
            whole((F, L // STEP)),
        ],
        out_specs=pl.BlockSpec((F, GROUP * 128), lambda i: (0, i)),
        scratch_shapes=[
            pltpu.VMEM((2 * F, L), jnp.bfloat16),
            pltpu.VMEM((F + 16, lanes), jnp.float32),
        ],
        compiler_params=pltpu.CompilerParams(vmem_limit_bytes=48 << 20),
    )(traces.reshape(WIN_DEV * CH_DEV, L), q, *fine, *coarse)


def cross_kernel(y_ref, idx_ref, band_ref, fold_ref, x):
    low = lax.broadcasted_iota(jnp.int32, (WINDOWS, 128), 1) < CH_DEV
    for m in range(N_CHAN // 2):
        even = y_ref[2 * m].astype(jnp.float32)
        odd = y_ref[2 * m + 1].astype(jnp.float32)
        lanes = slice(m * 128, m * 128 + 128)
        x[0:WINDOWS, lanes] = jnp.where(low, even, pltpu.roll(odd, CH_DEV, 1)).astype(jnp.bfloat16)
        x[WINDOWS : 2 * WINDOWS, lanes] = jnp.where(low, pltpu.roll(even, CH_DEV, 1), odd).astype(
            jnp.bfloat16
        )
    x[:, CHANNELS : CHANNELS + 128] = jnp.zeros((2 * WINDOWS, 128), jnp.bfloat16)

    low_out = lax.broadcasted_iota(jnp.int32, (128, 128), 1) < CH_DEV
    rows = lax.broadcasted_iota(jnp.int32, (128, 128), 0)
    lanes = lax.broadcasted_iota(jnp.int32, (128, 128), 1)
    mirror = jnp.where(rows + lanes == 127, 1.0, 0.0).astype(jnp.bfloat16)
    dims = (((0,), (0,)), ((), ()))
    for m in range(N_CHAN // 2):
        right = x[:, m * 128 : m * 128 + 256]
        left = jnp.dot(right[:, :128], mirror, preferred_element_type=jnp.float32)
        turned = jnp.concatenate([left[WINDOWS:], -left[:WINDOWS]], axis=0).astype(jnp.bfloat16)
        left = left.astype(jnp.bfloat16)
        cre = lax.dot_general(left, right, dims, preferred_element_type=jnp.float32)
        cim = lax.dot_general(turned, right, dims, preferred_element_type=jnp.float32)
        sre = pltpu.roll(cre, 128, 1, stride=1, stride_axis=0)[:, :128]
        sim = pltpu.roll(cim, 192, 1, stride=1, stride_axis=0)[:, :128]
        both = jnp.where(low_out, sre, sim).astype(jnp.bfloat16)
        for g in range(16):
            band_ref[16 * m + 15 - g] = both[g * ROWS : (g + 1) * ROWS]

    for g in range(CHANNELS // 256):
        wanted = idx_ref[:, g * 256 : g * 256 + 256]
        rows = lax.broadcasted_iota(jnp.int32, (CHANNELS, 256), 0)
        chosen = jnp.where(rows == wanted, 1.0, 0.0).astype(jnp.bfloat16)
        partner = jnp.dot(x[:, :CHANNELS], chosen, preferred_element_type=jnp.float32)
        own = x[:, g * 256 : g * 256 + 256].astype(jnp.float32)
        re_a, im_a = own[:WINDOWS], own[WINDOWS:]
        re_b, im_b = partner[:WINDOWS], partner[WINDOWS:]
        fold_ref[0:1, g * 256 : g * 256 + 256] = jnp.sum(
            re_a * re_b + im_a * im_b, axis=0, keepdims=True
        )
        fold_ref[1:2, g * 256 : g * 256 + 256] = jnp.sum(
            im_a * re_b - re_a * im_b, axis=0, keepdims=True
        )


def cross(y, idx):
    vmem = pl.BlockSpec(memory_space=pltpu.VMEM)
    return pl.pallas_call(
        cross_kernel,
        out_shape=(
            jax.ShapeDtypeStruct((F, ROWS, 128), jnp.bfloat16),
            jax.ShapeDtypeStruct((2, CHANNELS), jnp.float32),
        ),
        in_specs=[vmem, vmem],
        out_specs=(vmem, vmem),
        scratch_shapes=[pltpu.VMEM((2 * WINDOWS, CHANNELS + 128), jnp.bfloat16)],
        compiler_params=pltpu.CompilerParams(vmem_limit_bytes=48 << 20),
    )(y, idx)


def local(traces, quality, fold_block, fold_offset):
    sent = whiten(traces, quality).reshape(F, WIN_DEV, 128)
    got = lax.all_to_all(sent, ("chan", "win"), 0, 0, tiled=True)
    idx = (fold_block[:, 0] * CH_DEV + fold_offset)[None, :]
    band, fold = cross(got.reshape(N_CHAN, WINDOWS, 128), idx)
    band = band.reshape(N_CHAN, N_WIN, ROWS, 128)
    fold = fold.reshape(2, N_CHAN, CH_DEV).transpose(1, 0, 2).reshape(N_CHAN, 1, 1, 128)
    fold = jnp.broadcast_to(fold, (N_CHAN, N_WIN, SENT_ROWS - ROWS, 128)).astype(jnp.bfloat16)
    stacks = jnp.concatenate([band, fold], axis=2).reshape(F, SENT_ROWS, 128)
    stacks = lax.all_to_all(stacks, ("chan", "win"), 0, 0, tiled=True)
    stacks = stacks[:, : ROWS + 1, :].astype(jnp.float32)
    cosines, sines = inverse_table()
    factor = 1.0 / math.sqrt(F * WINDOWS)
    high = lax.Precision.HIGHEST
    lagged = jnp.einsum("fak,fl->akl", stacks[..., :REACH], cosines, precision=high)
    lagged += jnp.einsum("fak,fl->akl", stacks[..., REACH:], sines, precision=high)
    lagged *= factor
    own = lax.axis_index("win") * ROWS
    return lagged[:ROWS][::-1], lax.dynamic_slice_in_dim(lagged[ROWS], own, ROWS, 0)


def solution(mesh):
    in_specs = (P("win", "chan", None), P("chan"), P(), P())
    out_specs = (P(("chan", "win"), None, None), P(("chan", "win"), None))
    return jax.shard_map(local, mesh=mesh, in_specs=in_specs, out_specs=out_specs, check_vma=False)
```

```python
import math

import jax
import jax.numpy as jnp
import ml_dtypes
import numpy as np
from jax import lax
from jax.experimental import pallas as pl
from jax.experimental.pallas import tpu as pltpu
from jax.sharding import PartitionSpec as P

F = 256
BAND_LO = 32
NLAG = 256
REACH = 64
L = 4096
CH_DEV = 64
CHANNELS = 2048
WINDOWS = 96
N_CHAN = 32
N_WIN = 8
DEVICES = N_CHAN * N_WIN
WIN_DEV = WINDOWS // N_WIN
ROWS = CHANNELS // DEVICES
SMOOTH = 4
STEP = 128
GROUP = 4
CHUNKS = WIN_DEV // GROUP
LANES = GROUP * CH_DEV
MESH = pl.DeviceIdType.MESH
BF16 = jnp.bfloat16
F32 = jnp.float32


def forward_phases():
    frequency = np.arange(F, dtype=np.int64)[:, None] + BAND_LO
    fine = np.arange(STEP, dtype=np.int64)
    coarse = np.arange(L // STEP, dtype=np.int64) * STEP
    tables = []
    for steps in (fine, coarse):
        angles = (frequency * steps[None, :] % L).astype(np.float64) * (2.0 * math.pi / L)
        tables += [np.cos(angles), np.sin(angles)]
    joined = np.concatenate(tables, axis=1).astype(np.float32)
    return np.pad(joined, ((0, 0), (0, -joined.shape[1] % 128)))


def inverse_halves():
    shifts = np.arange(NLAG, dtype=np.int64)[None, :] + NLAG // 2
    frequency = np.arange(F, dtype=np.int64)[:, None] + BAND_LO
    angles = (frequency * shifts % NLAG).astype(np.float64) * (2.0 * math.pi / NLAG)
    factor = 1.0 / math.sqrt(F * WINDOWS)
    halves = []
    for part in (np.cos(angles) * factor, -np.sin(angles) * factor):
        high = part.astype(np.float32).astype(ml_dtypes.bfloat16)
        low = (part - high.astype(np.float64)).astype(np.float32).astype(ml_dtypes.bfloat16)
        halves += [high, low]
    return np.stack(halves)


def kernel(
    x_hbm, q_ref, idx_ref, phase_hbm, inverse_hbm, near_ref, fold_ref,
    xs, phase, inverse, table, energy, staged, sent, got, x, chosen_rows, band, folded, band_in, folded_in, flat, flat_fold, lag_in, turned_fold,
    in_sems, own_sem, send_sem, recv_sem, band_send, band_recv, fold_send, fold_recv,
):
    chan, win = lax.axis_index("chan"), lax.axis_index("win")
    me = chan * N_WIN + win

    def place(other):
        return (other // N_WIN, lax.rem(other, N_WIN))

    phase_copy = pltpu.make_async_copy(phase_hbm, phase, in_sems.at[CHUNKS])
    phase_copy.start()
    x_copies = [
        pltpu.make_async_copy(x_hbm.at[pl.ds(i * LANES, LANES)], xs.at[i], in_sems.at[i])
        for i in range(CHUNKS)
    ]
    for copy in x_copies:
        copy.start()
    inverse_copy = pltpu.make_async_copy(inverse_hbm, inverse, in_sems.at[CHUNKS + 1])
    inverse_copy.start()

    barrier = pltpu.get_barrier_semaphore()

    def greet(step, _):
        other = lax.rem(me + step, DEVICES)
        pl.semaphore_signal(barrier, inc=1, device_id=place(other), device_id_type=MESH)
        return 0

    lax.fori_loop(1, DEVICES, greet, 0)

    phase_copy.wait()
    coarse_at = 2 * STEP
    blocks = L // STEP
    fine_cos, fine_sin = phase[:, 0:STEP], phase[:, STEP : 2 * STEP]
    for block in range(blocks):
        cos_b = phase[:, coarse_at + block : coarse_at + block + 1]
        sin_b = phase[:, coarse_at + blocks + block : coarse_at + blocks + block + 1]
        lanes = slice(block * STEP, (block + 1) * STEP)
        table[0:F, lanes] = (fine_cos * cos_b - fine_sin * sin_b).astype(BF16)
        table[F : 2 * F, lanes] = (-fine_sin * cos_b - fine_cos * sin_b).astype(BF16)
    energy[0:8, :] = jnp.zeros((8, LANES), F32)
    energy[8 + F : 16 + F, :] = jnp.zeros((8, LANES), F32)

    low = lax.broadcasted_iota(jnp.int32, (F, 128), 1) < CH_DEV
    for i in range(CHUNKS):
        x_copies[i].wait()
        spectra = lax.dot_general(
            table[...], xs[i], (((1,), (1,)), ((), ())), preferred_element_type=F32
        )
        re, im = spectra[0:F], spectra[F : 2 * F]
        power = re * re + im * im
        energy[8 : 8 + F, :] = power
        smooth = power
        for shift in range(1, SMOOTH + 1):
            smooth = smooth + (
                energy[8 - shift : 8 - shift + F, :] + energy[8 + shift : 8 + shift + F, :]
            )
        water = jnp.sum(power, axis=0, keepdims=True) * (1.0 / F)
        scaling = lax.rsqrt(smooth * (1.0 / (2 * SMOOTH + 1)) + 0.1 * water + 1e-06) * q_ref[...]
        re, im = re * scaling, im * scaling
        for pair in range(GROUP // 2):
            re_p = re[:, pair * 128 : pair * 128 + 128]
            im_p = im[:, pair * 128 : pair * 128 + 128]
            first = jnp.where(low, re_p, pltpu.roll(im_p, CH_DEV, 1))
            second = jnp.where(low, pltpu.roll(re_p, CH_DEV, 1), im_p)
            staged[pl.ds(2 * pair, F, stride=GROUP), :] = first
            staged[pl.ds(2 * pair + 1, F, stride=GROUP), :] = second
        sent[:, i] = staged[...].reshape(F, GROUP, 128).astype(BF16)

    pl.semaphore_wait(barrier, DEVICES - 1)
    own_copy = pltpu.make_async_copy(sent.at[me], got.at[me], own_sem)
    own_copy.start()

    def send_spectra(step, _):
        other = lax.rem(me + step, DEVICES)
        pltpu.make_async_remote_copy(
            sent.at[other], got.at[me], send_sem, recv_sem,
            device_id=place(other), device_id_type=MESH,
        ).start()
        return 0

    lax.fori_loop(1, DEVICES, send_spectra, 0)
    own_copy.wait()

    def all_of(source, target, send, recv):
        some = pl.ds(0, DEVICES - 1)
        return pltpu.make_async_remote_copy(
            source.at[some], target.at[some], send, recv, device_id=place(lax.rem(me + 1, DEVICES)), device_id_type=MESH
        )

    spectra_copies = all_of(sent, got, send_sem, recv_sem)
    spectra_copies.wait_recv()

    low_w = lax.broadcasted_iota(jnp.int32, (WINDOWS, 128), 1) < CH_DEV

    def unpack(m, _):
        even = got[pl.ds(2 * N_WIN * m, N_WIN)].astype(F32).reshape(WINDOWS, 128)
        odd = got[pl.ds(2 * N_WIN * m + N_WIN, N_WIN)].astype(F32).reshape(WINDOWS, 128)
        lanes = pl.ds(pl.multiple_of(m * 128, 128), 128)
        x[0:WINDOWS, lanes] = jnp.where(low_w, even, pltpu.roll(odd, CH_DEV, 1)).astype(BF16)
        x[WINDOWS : 2 * WINDOWS, lanes] = jnp.where(low_w, pltpu.roll(even, CH_DEV, 1), odd).astype(BF16)
        return 0

    lax.fori_loop(0, N_CHAN // 2, unpack, 0)
    x[:, CHANNELS : CHANNELS + 128] = jnp.zeros((2 * WINDOWS, 128), BF16)

    low_1 = lax.broadcasted_iota(jnp.int32, (2, 128), 1) < CH_DEV

    def fold_block(g, _):
        lanes = pl.ds(pl.multiple_of(g * 256, 256), 256)
        wanted = idx_ref[:, lanes]
        rows = lax.broadcasted_iota(jnp.int32, (CHANNELS, 256), 0)
        chosen_rows[...] = jnp.where(rows == wanted, 1.0, 0.0).astype(BF16)
        partner = jnp.dot(x[:, 0:CHANNELS], chosen_rows[...], preferred_element_type=F32)
        own = x[:, lanes].astype(F32)
        re_a, im_a = own[:WINDOWS], own[WINDOWS:]
        re_b, im_b = partner[:WINDOWS], partner[WINDOWS:]
        re_c = jnp.sum(re_a * re_b + im_a * im_b, axis=0, keepdims=True)
        im_c = jnp.sum(im_a * re_b - re_a * im_b, axis=0, keepdims=True)
        re_c = jnp.broadcast_to(re_c, (2, 256))
        im_c = jnp.broadcast_to(im_c, (2, 256))
        for pair in range(2):
            re_p = re_c[:, pair * 128 : pair * 128 + 128]
            im_p = im_c[:, pair * 128 : pair * 128 + 128]
            even = jnp.where(low_1, re_p, pltpu.roll(im_p, CH_DEV, 1)).astype(BF16)
            odd = jnp.where(low_1, pltpu.roll(re_p, CH_DEV, 1), im_p).astype(BF16)
            folded[4 * g + 2 * pair] = even
            folded[4 * g + 2 * pair + 1] = odd
        return 0

    lax.fori_loop(0, CHANNELS // 256, fold_block, 0)

    own_copy = pltpu.make_async_copy(folded.at[chan], folded_in.at[me], own_sem)
    own_copy.start()

    def send_fold(step, _):
        other = lax.rem(me + step, DEVICES)
        pltpu.make_async_remote_copy(
            folded.at[other // N_WIN], folded_in.at[me], fold_send, fold_recv,
            device_id=place(other), device_id_type=MESH,
        ).start()
        return 0

    lax.fori_loop(1, DEVICES, send_fold, 0)
    own_copy.wait()

    low_out = lax.broadcasted_iota(jnp.int32, (128, 128), 1) < CH_DEV
    row_ids = lax.broadcasted_iota(jnp.int32, (128, 128), 0)
    lane_ids = lax.broadcasted_iota(jnp.int32, (128, 128), 1)
    mirror = jnp.where(row_ids + lane_ids == 127, 1.0, 0.0).astype(BF16)
    over_rows = (((0,), (0,)), ((), ()))

    def near(m, _):
        right = x[:, pl.ds(pl.multiple_of(m * 128, 128), 256)]
        left = jnp.dot(right[:, :128], mirror, preferred_element_type=F32)
        turned = jnp.concatenate([left[WINDOWS:], -left[:WINDOWS]], axis=0).astype(BF16)
        left = left.astype(BF16)
        re = lax.dot_general(left, right, over_rows, preferred_element_type=F32)
        im = lax.dot_general(turned, right, over_rows, preferred_element_type=F32)
        re = pltpu.roll(re, 128, 1, stride=1, stride_axis=0)[:, :128]
        im = pltpu.roll(im, 192, 1, stride=1, stride_axis=0)[:, :128]
        both = jnp.where(low_out, re, im).astype(BF16)
        for g in range(128 // ROWS):
            band[16 * m + 15 - g] = both[g * ROWS : (g + 1) * ROWS]
        return 0

    lax.fori_loop(0, N_CHAN // 2, near, 0)

    own_copy = pltpu.make_async_copy(band.at[me], band_in.at[me], own_sem)
    own_copy.start()

    def send_band(step, _):
        other = lax.rem(me + step, DEVICES)
        pltpu.make_async_remote_copy(
            band.at[other], band_in.at[me], band_send, band_recv,
            device_id=place(other), device_id_type=MESH,
        ).start()
        return 0

    lax.fori_loop(1, DEVICES, send_band, 0)
    own_copy.wait()

    inverse_copy.wait()
    spectra_copies.wait_send()
    fold_copies = all_of(folded_in, folded_in, fold_send, fold_recv)
    fold_copies.wait_send()
    fold_copies.wait_recv()
    band_copies = all_of(band, band_in, band_send, band_recv)
    band_copies.wait_send()
    band_copies.wait_recv()

    flat[...] = band_in[...].astype(F32).reshape(DEVICES * ROWS, 128)
    for r in range(ROWS):
        turned = flat[pl.ds(r, F, stride=ROWS), :].T
        at = (ROWS - 1 - r) * REACH
        lag_in[0, at : at + REACH, :] = turned[:REACH].astype(BF16)
        lag_in[1, at : at + REACH, :] = turned[REACH:].astype(BF16)
    flat_fold[...] = folded_in[...].astype(F32).reshape(DEVICES * 2, 128)
    turned_fold[...] = flat_fold[pl.ds(0, F, stride=2), :].T
    own = pl.multiple_of(win * ROWS, ROWS)
    pad = jnp.zeros((ROWS, F), F32)
    end = ROWS * REACH
    for part in range(2):
        mine = turned_fold[pl.ds(part * CH_DEV + own, ROWS), :]
        lag_in[part, end : end + 2 * ROWS, :] = jnp.concatenate([mine, pad], axis=0).astype(BF16)
    lagged = jnp.zeros((end + 2 * ROWS, NLAG), F32)
    for part in range(2):
        for half in range(2):
            lagged += jnp.dot(lag_in[part], inverse[2 * part + half], preferred_element_type=F32)
    near_ref[...] = lagged[:end].reshape(ROWS, REACH, NLAG)
    fold_ref[...] = lagged[end : end + ROWS]


def local(traces, quality, fold_block, fold_offset):
    vmem = pl.BlockSpec(memory_space=pltpu.VMEM)
    anywhere = pl.BlockSpec(memory_space=pl.ANY)
    q = jnp.tile(quality.astype(F32), GROUP)[None, :]
    idx = (fold_block[:, 0] * CH_DEV + fold_offset)[None, :]
    phases, inverse = forward_phases(), inverse_halves()
    sem = pltpu.SemaphoreType.DMA
    return pl.pallas_call(
        kernel,
        out_shape=(
            jax.ShapeDtypeStruct((ROWS, REACH, NLAG), F32),
            jax.ShapeDtypeStruct((ROWS, NLAG), F32),
        ),
        in_specs=[anywhere, vmem, vmem, anywhere, anywhere],
        out_specs=(vmem, vmem),
        scratch_shapes=[
            pltpu.VMEM((CHUNKS, LANES, L), BF16),
            pltpu.VMEM(phases.shape, F32),
            pltpu.VMEM(inverse.shape, BF16),
            pltpu.VMEM((2 * F, L), BF16),
            pltpu.VMEM((F + 16, LANES), F32),
            pltpu.VMEM((F * GROUP, 128), F32),
            pltpu.VMEM((DEVICES, CHUNKS, GROUP, 128), BF16),
            pltpu.VMEM((DEVICES, CHUNKS, GROUP, 128), BF16),
            pltpu.VMEM((2 * WINDOWS, CHANNELS + 128), BF16),
            pltpu.VMEM((CHANNELS, 256), BF16),
            pltpu.VMEM((DEVICES, ROWS, 128), BF16),
            pltpu.VMEM((N_CHAN, 2, 128), BF16),
            pltpu.VMEM((DEVICES, ROWS, 128), BF16),
            pltpu.VMEM((DEVICES, 2, 128), BF16),
            pltpu.VMEM((DEVICES * ROWS, 128), F32),
            pltpu.VMEM((DEVICES * 2, 128), F32),
            pltpu.VMEM((2, ROWS * REACH + 2 * ROWS, F), BF16),
            pltpu.VMEM((128, F), F32),
            sem((CHUNKS + 2,)),
            sem, sem, sem, sem, sem, sem, sem,
        ],
        compiler_params=pltpu.CompilerParams(
            vmem_limit_bytes=50 << 20, collective_id=0, has_side_effects=True
        ),
    )(traces.reshape(WIN_DEV * CH_DEV, L), q, idx, phases, inverse)


def solution(mesh):
    in_specs = (P("win", "chan", None), P("chan"), P(), P())
    out_specs = (P(("chan", "win"), None, None), P(("chan", "win"), None))
    return jax.shard_map(local, mesh=mesh, in_specs=in_specs, out_specs=out_specs, check_vma=False)
```

```python
import math

import jax
import jax.numpy as jnp
import ml_dtypes
import numpy as np
from jax import lax
from jax.experimental import pallas as pl
from jax.experimental.pallas import tpu as pltpu
from jax.sharding import PartitionSpec as P

F = 256
BAND_LO = 32
NLAG = 256
REACH = 64
L = 4096
CH_DEV = 64
CHANNELS = 2048
WINDOWS = 96
N_CHAN = 32
N_WIN = 8
DEVICES = N_CHAN * N_WIN
WIN_DEV = WINDOWS // N_WIN
ROWS = CHANNELS // DEVICES
SMOOTH = 4
STEP = 128
GROUP = 4
CHUNKS = WIN_DEV // GROUP
LANES = GROUP * CH_DEV
PAIR = 2 * N_WIN
PAIRS = DEVICES // PAIR
MESH = pl.DeviceIdType.MESH
BF16 = jnp.bfloat16
F32 = jnp.float32


def forward_phases():
    frequency = np.arange(F, dtype=np.int64)[:, None] + BAND_LO
    fine = np.arange(STEP, dtype=np.int64)
    coarse = np.arange(L // STEP, dtype=np.int64) * STEP
    tables = []
    for steps in (fine, coarse):
        angles = (frequency * steps[None, :] % L).astype(np.float64) * (2.0 * math.pi / L)
        tables += [np.cos(angles), np.sin(angles)]
    joined = np.concatenate(tables, axis=1).astype(np.float32)
    return np.pad(joined, ((0, 0), (0, -joined.shape[1] % 128)))


def inverse_halves():
    shifts = np.arange(NLAG, dtype=np.int64)[None, :] + NLAG // 2
    frequency = np.arange(F, dtype=np.int64)[:, None] + BAND_LO
    angles = (frequency * shifts % NLAG).astype(np.float64) * (2.0 * math.pi / NLAG)
    factor = 1.0 / math.sqrt(F * WINDOWS)
    halves = []
    for part in (np.cos(angles) * factor, -np.sin(angles) * factor):
        high = part.astype(np.float32).astype(ml_dtypes.bfloat16)
        low = (part - high.astype(np.float64)).astype(np.float32).astype(ml_dtypes.bfloat16)
        halves += [high, low]
    return np.stack(halves)


def kernel(
    x_hbm, q_hbm, block_hbm, offset_hbm, phase_hbm, inverse_hbm, near_ref, fold_ref,
    xs, quality, fold_block, fold_offset, phase, inverse, table, energy, staged, sent, got, x, chosen,
    band, folded, band_in, folded_in, flat, flat_fold, lag_in, turned_fold,
    x_sems, in_sems, own_sem, send_sem, recv_sems, band_send, band_recv, fold_send, fold_recv,
):
    chan, win = lax.axis_index("chan"), lax.axis_index("win")
    me = chan * N_WIN + win

    def place(other):
        return (other // N_WIN, lax.rem(other, N_WIN))

    small_copies = [
        pltpu.make_async_copy(source, target, in_sems.at[i])
        for i, (source, target) in enumerate(
            [
                (phase_hbm, phase),
                (q_hbm, quality),
                (block_hbm, fold_block),
                (offset_hbm, fold_offset),
                (inverse_hbm, inverse),
            ]
        )
    ]
    x_copies = [
        pltpu.make_async_copy(x_hbm.at[pl.ds(i * LANES, LANES)], xs.at[i], x_sems.at[i])
        for i in range(CHUNKS)
    ]
    for copy in small_copies[:1] + x_copies + small_copies[1:]:
        copy.start()
    barrier = pltpu.get_barrier_semaphore()

    def greet(step, _):
        other = lax.rem(me + step, DEVICES)
        pl.semaphore_signal(barrier, inc=1, device_id=place(other), device_id_type=MESH)
        return 0

    lax.fori_loop(1, DEVICES, greet, 0)

    for copy in small_copies:
        copy.wait()
    coarse_at = 2 * STEP
    blocks = L // STEP
    fine_cos, fine_sin = phase[:, 0:STEP], phase[:, STEP : 2 * STEP]
    for block in range(blocks):
        cos_b = phase[:, coarse_at + block : coarse_at + block + 1]
        sin_b = phase[:, coarse_at + blocks + block : coarse_at + blocks + block + 1]
        lanes = slice(block * STEP, (block + 1) * STEP)
        table[0:F, lanes] = (fine_cos * cos_b - fine_sin * sin_b).astype(BF16)
        table[F : 2 * F, lanes] = (-fine_sin * cos_b - fine_cos * sin_b).astype(BF16)
    energy[0:8, :] = jnp.zeros((8, LANES), F32)
    energy[8 + F : 16 + F, :] = jnp.zeros((8, LANES), F32)

    low = lax.broadcasted_iota(jnp.int32, (F, 128), 1) < CH_DEV
    keep = jnp.concatenate([quality[...].astype(F32)] * GROUP, axis=1)
    for i in range(CHUNKS):
        x_copies[i].wait()
        spectra = lax.dot_general(
            table[...], xs[i], (((1,), (1,)), ((), ())), preferred_element_type=F32
        )
        re, im = spectra[0:F], spectra[F : 2 * F]
        power = re * re + im * im
        energy[8 : 8 + F, :] = power
        smooth = power
        for shift in range(1, SMOOTH + 1):
            smooth = smooth + (
                energy[8 - shift : 8 - shift + F, :] + energy[8 + shift : 8 + shift + F, :]
            )
        water = jnp.sum(power, axis=0, keepdims=True) * (1.0 / F)
        scaling = lax.rsqrt(smooth * (1.0 / (2 * SMOOTH + 1)) + 0.1 * water + 1e-06) * keep
        re, im = re * scaling, im * scaling
        for pair in range(GROUP // 2):
            re_p = re[:, pair * 128 : pair * 128 + 128]
            im_p = im[:, pair * 128 : pair * 128 + 128]
            first = jnp.where(low, re_p, pltpu.roll(im_p, CH_DEV, 1))
            second = jnp.where(low, pltpu.roll(re_p, CH_DEV, 1), im_p)
            staged[pl.ds(2 * pair, F, stride=GROUP), :] = first
            staged[pl.ds(2 * pair + 1, F, stride=GROUP), :] = second
        sent[:, i] = staged[...].reshape(F, GROUP, 128).astype(BF16)

    wanted_all = fold_block[...] * CH_DEV + fold_offset[...]
    fold_offset[...] = wanted_all

    def choose(g, _):
        lanes = pl.ds(pl.multiple_of(g * 256, 256), 256)
        rows = lax.broadcasted_iota(jnp.int32, (CHANNELS, 256), 0)
        chosen[:, lanes] = jnp.where(rows == fold_offset[:, lanes], 1.0, 0.0).astype(BF16)
        return 0

    lax.fori_loop(0, CHANNELS // 256, choose, 0)
    x[:, CHANNELS : CHANNELS + 128] = jnp.zeros((2 * WINDOWS, 128), BF16)

    pl.semaphore_wait(barrier, DEVICES - 1)

    pair, spot = me // PAIR, lax.rem(me, PAIR)
    own_copy = pltpu.make_async_copy(sent.at[me], got.at[me], recv_sems.at[pair])
    own_copy.start()

    def send_spectra(step, _):
        other = PAIR * lax.rem(pair + step // PAIR, PAIRS) + lax.rem(spot + step, PAIR)
        pltpu.make_async_remote_copy(
            sent.at[other], got.at[me], send_sem, recv_sems.at[pair],
            device_id=place(other), device_id_type=MESH,
        ).start()
        return 0

    lax.fori_loop(1, DEVICES, send_spectra, 0)

    def all_of(source, target, send, recv, count):
        some = pl.ds(0, count)
        return pltpu.make_async_remote_copy(
            source.at[some], target.at[some], send, recv,
            device_id=place(lax.rem(me + 1, DEVICES)), device_id_type=MESH,
        )

    low_w = lax.broadcasted_iota(jnp.int32, (WINDOWS, 128), 1) < CH_DEV
    low_out = lax.broadcasted_iota(jnp.int32, (128, 128), 1) < CH_DEV
    row_ids = lax.broadcasted_iota(jnp.int32, (128, 128), 0)
    lane_ids = lax.broadcasted_iota(jnp.int32, (128, 128), 1)
    mirror = jnp.where(row_ids + lane_ids == 127, 1.0, 0.0).astype(BF16)
    over_rows = (((0,), (0,)), ((), ()))

    def unpack(m):
        all_of(sent, got, send_sem, recv_sems.at[m], PAIR).wait_recv()
        even = got[pl.ds(PAIR * m, N_WIN)].astype(F32).reshape(WINDOWS, 128)
        odd = got[pl.ds(PAIR * m + N_WIN, N_WIN)].astype(F32).reshape(WINDOWS, 128)
        lanes = pl.ds(pl.multiple_of(m * 128, 128), 128)
        x[0:WINDOWS, lanes] = jnp.where(low_w, even, pltpu.roll(odd, CH_DEV, 1)).astype(BF16)
        x[WINDOWS : 2 * WINDOWS, lanes] = jnp.where(low_w, pltpu.roll(even, CH_DEV, 1), odd).astype(BF16)

    def near(m):
        right = x[:, pl.ds(pl.multiple_of(m * 128, 128), 256)]
        left = jnp.dot(right[:, :128], mirror, preferred_element_type=F32)
        turned = jnp.concatenate([left[WINDOWS:], -left[:WINDOWS]], axis=0).astype(BF16)
        left = left.astype(BF16)
        re = lax.dot_general(left, right, over_rows, preferred_element_type=F32)
        im = lax.dot_general(turned, right, over_rows, preferred_element_type=F32)
        re = pltpu.roll(re, 128, 1, stride=1, stride_axis=0)[:, :128]
        im = pltpu.roll(im, 192, 1, stride=1, stride_axis=0)[:, :128]
        both = jnp.where(low_out, re, im).astype(BF16)
        for g in range(PAIR):
            band[PAIR * m + PAIR - 1 - g] = both[g * ROWS : (g + 1) * ROWS]

    def send_band(m, first):
        for step in range(first, PAIR):
            other = PAIR * m + lax.rem(spot + step, PAIR)
            pltpu.make_async_remote_copy(
                band.at[other], band_in.at[me], band_send, band_recv,
                device_id=place(other), device_id_type=MESH,
            ).start()

    unpack(pair)

    def arrive(step, _):
        m = lax.rem(pair + PAIRS - step, PAIRS)
        unpack(m)
        near(m)
        send_band(m, 0)
        return 0

    lax.fori_loop(1, PAIRS, arrive, 0)
    near(pair)
    own_band = pltpu.make_async_copy(band.at[me], band_in.at[me], own_sem)
    own_band.start()
    send_band(pair, 1)

    low_1 = lax.broadcasted_iota(jnp.int32, (2, 128), 1) < CH_DEV

    def fold_group(g, _):
        lanes = pl.ds(pl.multiple_of(g * 256, 256), 256)
        partner = jnp.dot(x[:, 0:CHANNELS], chosen[:, lanes], preferred_element_type=F32)
        own = x[:, lanes].astype(F32)
        re_a, im_a = own[:WINDOWS], own[WINDOWS:]
        re_b, im_b = partner[:WINDOWS], partner[WINDOWS:]
        re_c = jnp.sum(re_a * re_b + im_a * im_b, axis=0, keepdims=True)
        im_c = jnp.sum(im_a * re_b - re_a * im_b, axis=0, keepdims=True)
        re_c = jnp.broadcast_to(re_c, (2, 256))
        im_c = jnp.broadcast_to(im_c, (2, 256))
        for half in range(2):
            re_p = re_c[:, half * 128 : half * 128 + 128]
            im_p = im_c[:, half * 128 : half * 128 + 128]
            even = jnp.where(low_1, re_p, pltpu.roll(im_p, CH_DEV, 1)).astype(BF16)
            odd = jnp.where(low_1, pltpu.roll(re_p, CH_DEV, 1), im_p).astype(BF16)
            folded[4 * g + 2 * half] = even
            folded[4 * g + 2 * half + 1] = odd
        return 0

    lax.fori_loop(0, CHANNELS // 256, fold_group, 0)

    own_band.wait()
    own_fold = pltpu.make_async_copy(folded.at[chan], folded_in.at[me], own_sem)
    own_fold.start()

    def send_fold(step, _):
        other = lax.rem(me + step, DEVICES)
        pltpu.make_async_remote_copy(
            folded.at[other // N_WIN], folded_in.at[me], fold_send, fold_recv,
            device_id=place(other), device_id_type=MESH,
        ).start()
        return 0

    lax.fori_loop(1, DEVICES, send_fold, 0)
    own_fold.wait()

    all_of(sent, got, send_sem, recv_sems.at[0], DEVICES - 1).wait_send()
    band_copies = all_of(band, band_in, band_send, band_recv, DEVICES - 1)
    band_copies.wait_send()
    band_copies.wait_recv()
    fold_copies = all_of(folded_in, folded_in, fold_send, fold_recv, DEVICES - 1)
    fold_copies.wait_send()
    fold_copies.wait_recv()

    flat[...] = band_in[...].astype(F32).reshape(DEVICES * ROWS, 128)
    for r in range(ROWS):
        turned = flat[pl.ds(r, F, stride=ROWS), :].T
        at = (ROWS - 1 - r) * REACH
        lag_in[0, at : at + REACH, :] = turned[:REACH].astype(BF16)
        lag_in[1, at : at + REACH, :] = turned[REACH:].astype(BF16)
    flat_fold[...] = folded_in[...].astype(F32).reshape(DEVICES * 2, 128)
    turned_fold[...] = flat_fold[pl.ds(0, F, stride=2), :].T
    own = pl.multiple_of(win * ROWS, ROWS)
    pad = jnp.zeros((ROWS, F), F32)
    end = ROWS * REACH
    for part in range(2):
        mine = turned_fold[pl.ds(part * CH_DEV + own, ROWS), :]
        lag_in[part, end : end + 2 * ROWS, :] = jnp.concatenate([mine, pad], axis=0).astype(BF16)
    lagged = jnp.zeros((end + 2 * ROWS, NLAG), F32)
    for part in range(2):
        for half in range(2):
            lagged += jnp.dot(lag_in[part], inverse[2 * part + half], preferred_element_type=F32)
    near_ref[...] = lagged[:end].reshape(ROWS, REACH, NLAG)
    fold_ref[...] = lagged[end : end + ROWS]


def local(traces, quality, fold_block, fold_offset):
    vmem = pl.BlockSpec(memory_space=pltpu.VMEM)
    hbm = pl.BlockSpec(memory_space=pltpu.MemorySpace.HBM)
    phases, inverse = forward_phases(), inverse_halves()
    sem = pltpu.SemaphoreType.DMA
    return pl.pallas_call(
        kernel,
        out_shape=(
            jax.ShapeDtypeStruct((ROWS, REACH, NLAG), F32),
            jax.ShapeDtypeStruct((ROWS, NLAG), F32),
        ),
        in_specs=[hbm] * 6,
        out_specs=(vmem, vmem),
        scratch_shapes=[
            pltpu.VMEM((CHUNKS, LANES, L), BF16),
            pltpu.VMEM((1, CH_DEV), jnp.int32),
            pltpu.VMEM((1, CHANNELS), jnp.int32),
            pltpu.VMEM((1, CHANNELS), jnp.int32),
            pltpu.VMEM(phases.shape, F32),
            pltpu.VMEM(inverse.shape, BF16),
            pltpu.VMEM((2 * F, L), BF16),
            pltpu.VMEM((F + 16, LANES), F32),
            pltpu.VMEM((F * GROUP, 128), F32),
            pltpu.VMEM((DEVICES, CHUNKS, GROUP, 128), BF16),
            pltpu.VMEM((DEVICES, CHUNKS, GROUP, 128), BF16),
            pltpu.VMEM((2 * WINDOWS, CHANNELS + 128), BF16),
            pltpu.VMEM((CHANNELS, CHANNELS), BF16),
            pltpu.VMEM((DEVICES, ROWS, 128), BF16),
            pltpu.VMEM((N_CHAN, 2, 128), BF16),
            pltpu.VMEM((DEVICES, ROWS, 128), BF16),
            pltpu.VMEM((DEVICES, 2, 128), BF16),
            pltpu.VMEM((DEVICES * ROWS, 128), F32),
            pltpu.VMEM((DEVICES * 2, 128), F32),
            pltpu.VMEM((2, ROWS * REACH + 2 * ROWS, F), BF16),
            pltpu.VMEM((128, F), F32),
            sem((CHUNKS,)),
            sem((5,)),
            sem,
            sem,
            sem((PAIRS,)),
            sem, sem, sem, sem,
        ],
        compiler_params=pltpu.CompilerParams(
            vmem_limit_bytes=63 << 20, collective_id=0, has_side_effects=True
        ),
    )(
        traces.reshape(WIN_DEV * CH_DEV, L),
        quality.reshape(1, CH_DEV),
        fold_block.reshape(1, CHANNELS),
        fold_offset.reshape(1, CHANNELS),
        phases,
        inverse,
    )


def solution(mesh):
    in_specs = (P("win", "chan", None), P("chan"), P(), P())
    out_specs = (P(("chan", "win"), None, None), P(("chan", "win"), None))
    return jax.shard_map(local, mesh=mesh, in_specs=in_specs, out_specs=out_specs, check_vma=False)
```

```python
import math

import jax
import jax.numpy as jnp
import ml_dtypes
import numpy as np
from jax import lax
from jax.experimental import pallas as pl
from jax.experimental.pallas import tpu as pltpu
from jax.sharding import PartitionSpec as P

F = 256
BAND_LO = 32
NLAG = 256
REACH = 64
L = 4096
CH_DEV = 64
CHANNELS = 2048
WINDOWS = 96
N_CHAN = 32
N_WIN = 8
DEVICES = N_CHAN * N_WIN
WIN_DEV = WINDOWS // N_WIN
ROWS = CHANNELS // DEVICES
SMOOTH = 4
STEP = 128
GROUP = 4
CHUNKS = WIN_DEV // GROUP
LANES = GROUP * CH_DEV
PAIR = 2 * N_WIN
PAIRS = DEVICES // PAIR
GREETED = 96
MESH = pl.DeviceIdType.MESH
BF16 = jnp.bfloat16
F32 = jnp.float32


def forward_phases():
    frequency = np.arange(F, dtype=np.int64)[:, None] + BAND_LO
    fine = np.arange(STEP, dtype=np.int64)
    coarse = np.arange(L // STEP, dtype=np.int64) * STEP
    tables = []
    for steps in (fine, coarse):
        angles = (frequency * steps[None, :] % L).astype(np.float64) * (2.0 * math.pi / L)
        tables += [np.cos(angles), np.sin(angles)]
    joined = np.concatenate(tables, axis=1).astype(np.float32)
    return np.pad(joined, ((0, 0), (0, -joined.shape[1] % 128)))


def inverse_halves():
    shifts = np.arange(NLAG, dtype=np.int64)[None, :] + NLAG // 2
    frequency = np.arange(F, dtype=np.int64)[:, None] + BAND_LO
    angles = (frequency * shifts % NLAG).astype(np.float64) * (2.0 * math.pi / NLAG)
    factor = 1.0 / math.sqrt(F * WINDOWS)
    halves = []
    for part in (np.cos(angles) * factor, -np.sin(angles) * factor):
        high = part.astype(np.float32).astype(ml_dtypes.bfloat16)
        low = (part - high.astype(np.float64)).astype(np.float32).astype(ml_dtypes.bfloat16)
        halves += [high, low]
    return np.stack(halves)


def kernel(
    x_hbm, q_hbm, block_hbm, offset_hbm, phase_hbm, inverse_hbm, near_ref, fold_ref,
    xs, quality, fold_block, fold_offset, phase, inverse, table, energy, staged, sent, got, x, chosen,
    band, folded, band_in, folded_in, flat, flat_fold, by_bin, lag_in, turned_fold,
    x_sems, in_sems, own_sems, send_sem, recv_sems, band_send, band_recv, fold_send, fold_recv, relay_send, relay_recv,
):
    chan, win = lax.axis_index("chan"), lax.axis_index("win")
    me = chan * N_WIN + win

    def place(other):
        return (other // N_WIN, lax.rem(other, N_WIN))

    small_copies = [
        pltpu.make_async_copy(source, target, in_sems.at[i])
        for i, (source, target) in enumerate(
            [
                (phase_hbm, phase),
                (q_hbm, quality),
                (block_hbm, fold_block),
                (offset_hbm, fold_offset),
                (inverse_hbm, inverse),
            ]
        )
    ]
    x_copies = [
        pltpu.make_async_copy(x_hbm.at[pl.ds(i * LANES, LANES)], xs.at[i], x_sems.at[i])
        for i in range(CHUNKS)
    ]
    for copy in small_copies[:4] + x_copies + small_copies[4:]:
        copy.start()
    barrier = pltpu.get_barrier_semaphore()

    def greet(step, _):
        other = lax.rem(me + step, DEVICES)
        pl.semaphore_signal(barrier, inc=1, device_id=place(other), device_id_type=MESH)
        return 0

    lax.fori_loop(1, GREETED, greet, 0)

    small_copies[0].wait()
    coarse_at = 2 * STEP
    blocks = L // STEP
    fine_cos, fine_sin = phase[:, 0:STEP], phase[:, STEP : 2 * STEP]
    for block in range(blocks):
        cos_b = phase[:, coarse_at + block : coarse_at + block + 1]
        sin_b = phase[:, coarse_at + blocks + block : coarse_at + blocks + block + 1]
        lanes = slice(block * STEP, (block + 1) * STEP)
        table[0:F, lanes] = (fine_cos * cos_b - fine_sin * sin_b).astype(BF16)
        table[F : 2 * F, lanes] = (-fine_sin * cos_b - fine_cos * sin_b).astype(BF16)
        for step in range(GREETED + block, DEVICES, blocks):
            greet(step, 0)
    energy[0:8, :] = jnp.zeros((8, LANES), F32)
    energy[8 + F : 16 + F, :] = jnp.zeros((8, LANES), F32)

    for copy in small_copies[1:4]:
        copy.wait()
    low = lax.broadcasted_iota(jnp.int32, (F, 128), 1) < CH_DEV
    keep = jnp.concatenate([quality[...].astype(F32)] * GROUP, axis=1)
    for i in range(CHUNKS):
        x_copies[i].wait()
        spectra = lax.dot_general(
            table[...], xs[i], (((1,), (1,)), ((), ())), preferred_element_type=F32
        )
        re, im = spectra[0:F], spectra[F : 2 * F]
        power = re * re + im * im
        energy[8 : 8 + F, :] = power
        smooth = power
        for shift in range(1, SMOOTH + 1):
            smooth = smooth + (
                energy[8 - shift : 8 - shift + F, :] + energy[8 + shift : 8 + shift + F, :]
            )
        water = jnp.sum(power, axis=0, keepdims=True) * (1.0 / F)
        scaling = lax.rsqrt(smooth * (1.0 / (2 * SMOOTH + 1)) + 0.1 * water + 1e-06) * keep
        re, im = re * scaling, im * scaling
        for pair in range(GROUP // 2):
            re_p = re[:, pair * 128 : pair * 128 + 128]
            im_p = im[:, pair * 128 : pair * 128 + 128]
            first = jnp.where(low, re_p, pltpu.roll(im_p, CH_DEV, 1))
            second = jnp.where(low, pltpu.roll(re_p, CH_DEV, 1), im_p)
            staged[pl.ds(2 * pair, F, stride=GROUP), :] = first
            staged[pl.ds(2 * pair + 1, F, stride=GROUP), :] = second
        sent[:, i] = staged[...].reshape(F, GROUP, 128).astype(BF16)

    pl.semaphore_wait(barrier, DEVICES - 1)

    pair, spot = me // PAIR, lax.rem(me, PAIR)
    own_copy = pltpu.make_async_copy(sent.at[me], got.at[me], recv_sems.at[pair])
    own_copy.start()

    def send_spectra(step, _):
        other = PAIR * lax.rem(pair + step // PAIR, PAIRS) + lax.rem(spot + step, PAIR)
        pltpu.make_async_remote_copy(
            sent.at[other], got.at[me], send_sem, recv_sems.at[pair],
            device_id=place(other), device_id_type=MESH,
        ).start()
        return 0

    lax.fori_loop(1, DEVICES, send_spectra, 0)

    wanted_all = fold_block[...] * CH_DEV + fold_offset[...]
    fold_offset[...] = wanted_all

    def choose(g, _):
        lanes = pl.ds(pl.multiple_of(g * 256, 256), 256)
        rows = lax.broadcasted_iota(jnp.int32, (CHANNELS, 256), 0)
        chosen[:, lanes] = jnp.where(rows == fold_offset[:, lanes], 1.0, 0.0).astype(BF16)
        return 0

    lax.fori_loop(0, CHANNELS // 256, choose, 0)
    x[:, CHANNELS : CHANNELS + 128] = jnp.zeros((2 * WINDOWS, 128), BF16)

    def all_of(source, target, send, recv, count):
        some = pl.ds(0, count)
        return pltpu.make_async_remote_copy(
            source.at[some], target.at[some], send, recv,
            device_id=place(lax.rem(me + 1, DEVICES)), device_id_type=MESH,
        )

    low_w = lax.broadcasted_iota(jnp.int32, (WINDOWS, 128), 1) < CH_DEV
    low_out = lax.broadcasted_iota(jnp.int32, (128, 128), 1) < CH_DEV
    row_ids = lax.broadcasted_iota(jnp.int32, (128, 128), 0)
    lane_ids = lax.broadcasted_iota(jnp.int32, (128, 128), 1)
    mirror = jnp.where(row_ids + lane_ids == 127, 1.0, 0.0).astype(BF16)
    over_rows = (((0,), (0,)), ((), ()))

    def unpack(m):
        all_of(sent, got, send_sem, recv_sems.at[m], PAIR).wait_recv()
        even = got[pl.ds(PAIR * m, N_WIN)].astype(F32).reshape(WINDOWS, 128)
        odd = got[pl.ds(PAIR * m + N_WIN, N_WIN)].astype(F32).reshape(WINDOWS, 128)
        lanes = pl.ds(pl.multiple_of(m * 128, 128), 128)
        x[0:WINDOWS, lanes] = jnp.where(low_w, even, pltpu.roll(odd, CH_DEV, 1)).astype(BF16)
        x[WINDOWS : 2 * WINDOWS, lanes] = jnp.where(low_w, pltpu.roll(even, CH_DEV, 1), odd).astype(BF16)

    def near(m):
        right = x[:, pl.ds(pl.multiple_of(m * 128, 128), 256)]
        left = jnp.dot(right[:, :128], mirror, preferred_element_type=F32)
        turned = jnp.concatenate([left[WINDOWS:], -left[:WINDOWS]], axis=0).astype(BF16)
        left = left.astype(BF16)
        re = lax.dot_general(left, right, over_rows, preferred_element_type=F32)
        im = lax.dot_general(turned, right, over_rows, preferred_element_type=F32)
        re = pltpu.roll(re, 128, 1, stride=1, stride_axis=0)[:, :128]
        im = pltpu.roll(im, 192, 1, stride=1, stride_axis=0)[:, :128]
        both = jnp.where(low_out, re, im).astype(BF16)
        for g in range(PAIR):
            band[PAIR * m + PAIR - 1 - g] = both[g * ROWS : (g + 1) * ROWS]

    def send_band(m, first):
        for step in range(first, PAIR):
            other = PAIR * m + lax.rem(spot + step, PAIR)
            pltpu.make_async_remote_copy(
                band.at[other], band_in.at[me], band_send, band_recv,
                device_id=place(other), device_id_type=MESH,
            ).start()

    unpack(pair)

    def arrive(step, _):
        m = lax.rem(pair + PAIRS - step, PAIRS)
        unpack(m)
        near(m)
        send_band(m, 0)
        return 0

    lax.fori_loop(1, PAIRS - 1, arrive, 0)
    last = lax.rem(pair + 1, PAIRS)
    unpack(last)

    low_1 = lax.broadcasted_iota(jnp.int32, (2, 128), 1) < CH_DEV

    def fold_group(g, _):
        lanes = pl.ds(pl.multiple_of(g * 256, 256), 256)
        partner = jnp.dot(x[:, 0:CHANNELS], chosen[:, lanes], preferred_element_type=F32)
        own = x[:, lanes].astype(F32)
        re_a, im_a = own[:WINDOWS], own[WINDOWS:]
        re_b, im_b = partner[:WINDOWS], partner[WINDOWS:]
        re_c = jnp.sum(re_a * re_b + im_a * im_b, axis=0, keepdims=True)
        im_c = jnp.sum(im_a * re_b - re_a * im_b, axis=0, keepdims=True)
        re_c = jnp.broadcast_to(re_c, (2, 256))
        im_c = jnp.broadcast_to(im_c, (2, 256))
        for half in range(2):
            re_p = re_c[:, half * 128 : half * 128 + 128]
            im_p = im_c[:, half * 128 : half * 128 + 128]
            even = jnp.where(low_1, re_p, pltpu.roll(im_p, CH_DEV, 1)).astype(BF16)
            odd = jnp.where(low_1, pltpu.roll(re_p, CH_DEV, 1), im_p).astype(BF16)
            folded[4 * g + 2 * half] = even
            folded[4 * g + 2 * half + 1] = odd
        return 0

    lax.fori_loop(0, CHANNELS // 256, fold_group, 0)

    own_fold = pltpu.make_async_copy(folded.at[chan], folded_in.at[win, chan], own_sems.at[0])
    own_fold.start()

    def send_fold(step, _):
        other = lax.rem(chan + step, N_CHAN)
        pltpu.make_async_remote_copy(
            folded.at[other], folded_in.at[win, chan], fold_send, fold_recv,
            device_id=(other, win), device_id_type=MESH,
        ).start()
        return 0

    lax.fori_loop(1, N_CHAN, send_fold, 0)

    near(last)
    send_band(last, 0)
    near(pair)
    own_band = pltpu.make_async_copy(band.at[me], band_in.at[me], own_sems.at[1])
    own_band.start()
    send_band(pair, 1)

    own_fold.wait()
    fold_copies = all_of(folded, folded, fold_send, fold_recv, N_CHAN - 1)
    fold_copies.wait_recv()

    def relay(step, _):
        pltpu.make_async_remote_copy(
            folded_in.at[win], folded_in.at[win], relay_send, relay_recv,
            device_id=(chan, lax.rem(win + step, N_WIN)), device_id_type=MESH,
        ).start()
        return 0

    lax.fori_loop(1, N_WIN, relay, 0)

    all_of(sent, got, send_sem, recv_sems.at[0], DEVICES - 1).wait_send()
    band_copies = all_of(band, band_in, band_send, band_recv, DEVICES - 1)
    band_copies.wait_send()
    band_copies.wait_recv()
    fold_copies.wait_send()
    relay_copies = all_of(folded_in, folded_in, relay_send, relay_recv, N_WIN - 1)
    relay_copies.wait_send()
    relay_copies.wait_recv()
    own_band.wait()
    small_copies[4].wait()

    flat[...] = band_in[...].astype(F32).reshape(DEVICES * ROWS, 128)
    for r in range(ROWS):
        turned = flat[pl.ds(r, F, stride=ROWS), :].T
        at = (ROWS - 1 - r) * REACH
        lag_in[0, at : at + REACH, :] = turned[:REACH].astype(BF16)
        lag_in[1, at : at + REACH, :] = turned[REACH:].astype(BF16)
    flat_fold[...] = folded_in[...].astype(F32).reshape(DEVICES * 2, 128)
    for w in range(N_WIN):
        rows = flat_fold[pl.ds(2 * N_CHAN * w, N_CHAN, stride=2), :]
        by_bin[pl.ds(w, N_CHAN, stride=N_WIN), :] = rows
    turned_fold[...] = by_bin[...].T
    own = pl.multiple_of(win * ROWS, ROWS)
    pad = jnp.zeros((ROWS, F), F32)
    end = ROWS * REACH
    for part in range(2):
        mine = turned_fold[pl.ds(part * CH_DEV + own, ROWS), :]
        lag_in[part, end : end + 2 * ROWS, :] = jnp.concatenate([mine, pad], axis=0).astype(BF16)
    lagged = jnp.zeros((end + 2 * ROWS, NLAG), F32)
    for part in range(2):
        for half in range(2):
            lagged += jnp.dot(lag_in[part], inverse[2 * part + half], preferred_element_type=F32)
    near_ref[...] = lagged[:end].reshape(ROWS, REACH, NLAG)
    fold_ref[...] = lagged[end : end + ROWS]


def local(traces, quality, fold_block, fold_offset):
    vmem = pl.BlockSpec(memory_space=pltpu.VMEM)
    hbm = pl.BlockSpec(memory_space=pltpu.MemorySpace.HBM)
    phases, inverse = forward_phases(), inverse_halves()
    sem = pltpu.SemaphoreType.DMA
    return pl.pallas_call(
        kernel,
        out_shape=(
            jax.ShapeDtypeStruct((ROWS, REACH, NLAG), F32),
            jax.ShapeDtypeStruct((ROWS, NLAG), F32),
        ),
        in_specs=[hbm] * 6,
        out_specs=(vmem, vmem),
        scratch_shapes=[
            pltpu.VMEM((CHUNKS, LANES, L), BF16),
            pltpu.VMEM((1, CH_DEV), jnp.int32),
            pltpu.VMEM((1, CHANNELS), jnp.int32),
            pltpu.VMEM((1, CHANNELS), jnp.int32),
            pltpu.VMEM(phases.shape, F32),
            pltpu.VMEM(inverse.shape, BF16),
            pltpu.VMEM((2 * F, L), BF16),
            pltpu.VMEM((F + 16, LANES), F32),
            pltpu.VMEM((F * GROUP, 128), F32),
            pltpu.VMEM((DEVICES, CHUNKS, GROUP, 128), BF16),
            pltpu.VMEM((DEVICES, CHUNKS, GROUP, 128), BF16),
            pltpu.VMEM((2 * WINDOWS, CHANNELS + 128), BF16),
            pltpu.VMEM((CHANNELS, CHANNELS), BF16),
            pltpu.VMEM((DEVICES, ROWS, 128), BF16),
            pltpu.VMEM((N_CHAN, 2, 128), BF16),
            pltpu.VMEM((DEVICES, ROWS, 128), BF16),
            pltpu.VMEM((N_WIN, N_CHAN, 2, 128), BF16),
            pltpu.VMEM((DEVICES * ROWS, 128), F32),
            pltpu.VMEM((DEVICES * 2, 128), F32),
            pltpu.VMEM((F, 128), F32),
            pltpu.VMEM((2, ROWS * REACH + 2 * ROWS, F), BF16),
            pltpu.VMEM((128, F), F32),
            sem((CHUNKS,)),
            sem((5,)),
            sem((2,)),
            sem,
            sem((PAIRS,)),
            sem, sem, sem, sem, sem, sem,
        ],
        compiler_params=pltpu.CompilerParams(
            vmem_limit_bytes=60 << 20, collective_id=0, has_side_effects=True
        ),
    )(
        traces.reshape(WIN_DEV * CH_DEV, L),
        quality.reshape(1, CH_DEV),
        fold_block.reshape(1, CHANNELS),
        fold_offset.reshape(1, CHANNELS),
        phases,
        inverse,
    )


def solution(mesh):
    in_specs = (P("win", "chan", None), P("chan"), P(), P())
    out_specs = (P(("chan", "win"), None, None), P(("chan", "win"), None))
    return jax.shard_map(local, mesh=mesh, in_specs=in_specs, out_specs=out_specs, check_vma=False)
```

```python
import math

import jax
import jax.numpy as jnp
import ml_dtypes
import numpy as np
from jax import lax
from jax.experimental import pallas as pl
from jax.experimental.pallas import tpu as pltpu
from jax.sharding import PartitionSpec as P

F = 256
BAND_LO = 32
NLAG = 256
REACH = 64
L = 4096
CH_DEV = 64
CHANNELS = 2048
WINDOWS = 96
N_CHAN = 32
N_WIN = 8
DEVICES = N_CHAN * N_WIN
WIN_DEV = WINDOWS // N_WIN
ROWS = CHANNELS // DEVICES
SMOOTH = 4
STEP = 128
GROUP = 4
CHUNKS = WIN_DEV // GROUP
LANES = GROUP * CH_DEV
PAIR = 2 * N_WIN
PAIRS = DEVICES // PAIR
GREETED = 13
MESH = pl.DeviceIdType.MESH
BF16 = jnp.bfloat16
F32 = jnp.float32


def forward_phases():
    frequency = np.arange(F, dtype=np.int64)[:, None] + BAND_LO
    fine = np.arange(STEP, dtype=np.int64)
    coarse = np.arange(L // STEP, dtype=np.int64) * STEP
    tables = []
    for steps in (fine, coarse):
        angles = (frequency * steps[None, :] % L).astype(np.float64) * (2.0 * math.pi / L)
        tables += [np.cos(angles), np.sin(angles)]
    joined = np.concatenate(tables, axis=1).astype(np.float32)
    return np.pad(joined, ((0, 0), (0, -joined.shape[1] % 128)))


def inverse_halves():
    shifts = np.arange(NLAG, dtype=np.int64)[None, :] + NLAG // 2
    frequency = np.arange(F, dtype=np.int64)[:, None] + BAND_LO
    angles = (frequency * shifts % NLAG).astype(np.float64) * (2.0 * math.pi / NLAG)
    halves = []
    for part in (np.cos(angles), -np.sin(angles)):
        high = part.astype(np.float32).astype(ml_dtypes.bfloat16)
        low = (part - high.astype(np.float64)).astype(np.float32).astype(ml_dtypes.bfloat16)
        halves += [high, low]
    return np.stack(halves)


def kernel(
    x_hbm, q_hbm, block_hbm, offset_hbm, phase_hbm, inverse_hbm, near_ref, fold_ref,
    xs, quality, fold_block, fold_offset, phase, inverse, table, energy, staged, sent, got, x, chosen,
    band, folded, band_in, folded_in, flat, flat_fold, by_bin, lag_in, turned_fold,
    x_sems, in_sems, own_sems, send_sem, recv_sems, band_send, band_recv, fold_send, fold_recv, relay_send, relay_recv,
):
    chan, win = lax.axis_index("chan"), lax.axis_index("win")
    me = chan * N_WIN + win

    wins = [lax.rem(win + k, N_WIN) for k in range(N_WIN)]
    side = lax.rem(chan, 2)
    sides = (side, 1 - side)
    neighbour = (lax.rem(chan + 1, N_CHAN), win)

    small_copies = [
        pltpu.make_async_copy(source, target, in_sems.at[i])
        for i, (source, target) in enumerate(
            [
                (phase_hbm, phase),
                (q_hbm, quality),
                (block_hbm, fold_block),
                (offset_hbm, fold_offset),
                (inverse_hbm, inverse),
            ]
        )
    ]
    x_copies = [
        pltpu.make_async_copy(x_hbm.at[pl.ds(i * LANES, LANES)], xs.at[i], x_sems.at[i])
        for i in range(CHUNKS)
    ]
    for copy in small_copies[:4] + x_copies + small_copies[4:]:
        copy.start()
    barrier = pltpu.get_barrier_semaphore()

    def greet(step, _):
        other = lax.rem(chan + step, N_CHAN)
        for k in range(N_WIN):
            pl.semaphore_signal(barrier, inc=1, device_id=(other, wins[k]), device_id_type=MESH)
        return 0

    for k in range(1, N_WIN):
        pl.semaphore_signal(barrier, inc=1, device_id=(chan, wins[k]), device_id_type=MESH)
    lax.fori_loop(1, GREETED, greet, 0)

    small_copies[0].wait()
    coarse_at = 2 * STEP
    blocks = L // STEP
    fine_cos, fine_sin = phase[:, 0:STEP], phase[:, STEP : 2 * STEP]
    for block in range(blocks):
        cos_b = phase[:, coarse_at + block : coarse_at + block + 1]
        sin_b = phase[:, coarse_at + blocks + block : coarse_at + blocks + block + 1]
        lanes = slice(block * STEP, (block + 1) * STEP)
        table[0:F, lanes] = (fine_cos * cos_b - fine_sin * sin_b).astype(BF16)
        table[F : 2 * F, lanes] = (-fine_sin * cos_b - fine_cos * sin_b).astype(BF16)
        if GREETED <= block < N_CHAN:
            greet(block, 0)
    energy[0:8, :] = jnp.zeros((8, LANES), F32)
    energy[8 + F : 16 + F, :] = jnp.zeros((8, LANES), F32)

    for copy in small_copies[1:4]:
        copy.wait()
    low = lax.broadcasted_iota(jnp.int32, (F, 128), 1) < CH_DEV
    keep = jnp.concatenate([quality[...].astype(F32)] * GROUP, axis=1)
    for i in range(CHUNKS):
        x_copies[i].wait()
        spectra = lax.dot_general(
            table[...], xs[i], (((1,), (1,)), ((), ())), preferred_element_type=F32
        )
        re, im = spectra[0:F], spectra[F : 2 * F]
        power = re * re + im * im
        energy[8 : 8 + F, :] = power
        smooth = power
        for shift in range(1, SMOOTH + 1):
            smooth = smooth + (
                energy[8 - shift : 8 - shift + F, :] + energy[8 + shift : 8 + shift + F, :]
            )
        water = jnp.sum(power, axis=0, keepdims=True) * (1.0 / F)
        scaling = lax.rsqrt(smooth * (1.0 / (2 * SMOOTH + 1)) + 0.1 * water + 1e-06) * keep
        re, im = re * scaling, im * scaling
        for pair in range(GROUP // 2):
            re_p = re[:, pair * 128 : pair * 128 + 128]
            im_p = im[:, pair * 128 : pair * 128 + 128]
            first = jnp.where(low, re_p, pltpu.roll(im_p, CH_DEV, 1))
            second = jnp.where(low, pltpu.roll(re_p, CH_DEV, 1), im_p)
            staged[pl.ds(2 * pair, F, stride=GROUP), :] = first
            staged[pl.ds(2 * pair + 1, F, stride=GROUP), :] = second
        sent[:, i] = staged[...].reshape(F, GROUP, 128).astype(BF16)

    pl.semaphore_wait(barrier, DEVICES - 1)

    pair = chan // 2
    own_copy = pltpu.make_async_copy(sent.at[me], got.at[me], recv_sems.at[pair])
    own_copy.start()

    def send_to(source, target, send, recv, m, own):
        for h in range(2):
            other = 2 * m + sides[h]
            for k in range(1 if own and h == 0 else 0, N_WIN):
                pltpu.make_async_remote_copy(
                    source.at[other * N_WIN + wins[k]], target.at[me], send, recv,
                    device_id=(other, wins[k]), device_id_type=MESH,
                ).start()

    def send_spectra(step, _):
        m = lax.rem(pair + step, PAIRS)
        send_to(sent, got, send_sem, recv_sems.at[pair], m, False)
        return 0

    send_to(sent, got, send_sem, recv_sems.at[pair], pair, True)
    lax.fori_loop(1, PAIRS, send_spectra, 0)

    wanted_all = fold_block[...] * CH_DEV + fold_offset[...]
    fold_offset[...] = wanted_all

    def choose(g, _):
        lanes = pl.ds(pl.multiple_of(g * 256, 256), 256)
        rows = lax.broadcasted_iota(jnp.int32, (CHANNELS, 256), 0)
        chosen[:, lanes] = jnp.where(rows == fold_offset[:, lanes], 1.0, 0.0).astype(BF16)
        return 0

    lax.fori_loop(0, CHANNELS // 256, choose, 0)
    x[:, CHANNELS : CHANNELS + 128] = jnp.zeros((2 * WINDOWS, 128), BF16)

    def all_of(source, target, send, recv, count):
        some = pl.ds(0, count)
        return pltpu.make_async_remote_copy(
            source.at[some], target.at[some], send, recv,
            device_id=neighbour, device_id_type=MESH,
        )

    low_w = lax.broadcasted_iota(jnp.int32, (WINDOWS, 128), 1) < CH_DEV
    low_out = lax.broadcasted_iota(jnp.int32, (128, 128), 1) < CH_DEV
    row_ids = lax.broadcasted_iota(jnp.int32, (128, 128), 0)
    lane_ids = lax.broadcasted_iota(jnp.int32, (128, 128), 1)
    mirror = jnp.where(row_ids + lane_ids == 127, 1.0, 0.0).astype(BF16)
    over_rows = (((0,), (0,)), ((), ()))

    def unpack(m):
        all_of(sent, got, send_sem, recv_sems.at[m], PAIR).wait_recv()
        even = got[pl.ds(PAIR * m, N_WIN)].astype(F32).reshape(WINDOWS, 128)
        odd = got[pl.ds(PAIR * m + N_WIN, N_WIN)].astype(F32).reshape(WINDOWS, 128)
        lanes = pl.ds(pl.multiple_of(m * 128, 128), 128)
        x[0:WINDOWS, lanes] = jnp.where(low_w, even, pltpu.roll(odd, CH_DEV, 1)).astype(BF16)
        x[WINDOWS : 2 * WINDOWS, lanes] = jnp.where(low_w, pltpu.roll(even, CH_DEV, 1), odd).astype(BF16)

    def near(m):
        right = x[:, pl.ds(pl.multiple_of(m * 128, 128), 256)]
        left = jnp.dot(right[:, :128], mirror, preferred_element_type=F32)
        turned = jnp.concatenate([left[WINDOWS:], -left[:WINDOWS]], axis=0).astype(BF16)
        left = left.astype(BF16)
        re = lax.dot_general(left, right, over_rows, preferred_element_type=F32)
        im = lax.dot_general(turned, right, over_rows, preferred_element_type=F32)
        re = pltpu.roll(re, 128, 1, stride=1, stride_axis=0)[:, :128]
        im = pltpu.roll(im, 192, 1, stride=1, stride_axis=0)[:, :128]
        both = jnp.where(low_out, re, im).astype(BF16)
        for g in range(PAIR):
            band[PAIR * m + PAIR - 1 - g] = both[g * ROWS : (g + 1) * ROWS]

    def send_band(m, own):
        send_to(band, band_in, band_send, band_recv, m, own)

    unpack(pair)

    def arrive(step, _):
        m = lax.rem(pair + PAIRS - step, PAIRS)
        unpack(m)
        near(m)
        send_band(m, False)
        return 0

    lax.fori_loop(1, PAIRS - 1, arrive, 0)
    last = lax.rem(pair + 1, PAIRS)
    unpack(last)

    low_1 = lax.broadcasted_iota(jnp.int32, (2, 128), 1) < CH_DEV

    def fold_group(g, _):
        lanes = pl.ds(pl.multiple_of(g * 256, 256), 256)
        partner = jnp.dot(x[:, 0:CHANNELS], chosen[:, lanes], preferred_element_type=F32)
        own = x[:, lanes].astype(F32)
        re_a, im_a = own[:WINDOWS], own[WINDOWS:]
        re_b, im_b = partner[:WINDOWS], partner[WINDOWS:]
        re_c = jnp.sum(re_a * re_b + im_a * im_b, axis=0, keepdims=True)
        im_c = jnp.sum(im_a * re_b - re_a * im_b, axis=0, keepdims=True)
        re_c = jnp.broadcast_to(re_c, (2, 256))
        im_c = jnp.broadcast_to(im_c, (2, 256))
        for half in range(2):
            re_p = re_c[:, half * 128 : half * 128 + 128]
            im_p = im_c[:, half * 128 : half * 128 + 128]
            even = jnp.where(low_1, re_p, pltpu.roll(im_p, CH_DEV, 1)).astype(BF16)
            odd = jnp.where(low_1, pltpu.roll(re_p, CH_DEV, 1), im_p).astype(BF16)
            folded[4 * g + 2 * half] = even
            folded[4 * g + 2 * half + 1] = odd
        return 0

    lax.fori_loop(0, CHANNELS // 256, fold_group, 0)

    own_fold = pltpu.make_async_copy(folded.at[chan], folded_in.at[win, chan], own_sems.at[0])
    own_fold.start()

    def send_fold(step, _):
        other = lax.rem(chan + step, N_CHAN)
        pltpu.make_async_remote_copy(
            folded.at[other], folded_in.at[win, chan], fold_send, fold_recv,
            device_id=(other, win), device_id_type=MESH,
        ).start()
        return 0

    lax.fori_loop(1, N_CHAN, send_fold, 0)

    near(last)
    send_band(last, False)
    near(pair)
    own_band = pltpu.make_async_copy(band.at[me], band_in.at[me], own_sems.at[1])
    own_band.start()
    send_band(pair, True)

    own_fold.wait()
    fold_copies = all_of(folded, folded, fold_send, fold_recv, N_CHAN - 1)
    fold_copies.wait_recv()

    def relay(step, _):
        pltpu.make_async_remote_copy(
            folded_in.at[win], folded_in.at[win], relay_send, relay_recv,
            device_id=(chan, lax.rem(win + step, N_WIN)), device_id_type=MESH,
        ).start()
        return 0

    lax.fori_loop(1, N_WIN, relay, 0)

    all_of(sent, got, send_sem, recv_sems.at[0], DEVICES - 1).wait_send()
    band_copies = all_of(band, band_in, band_send, band_recv, DEVICES - 1)
    band_copies.wait_send()
    band_copies.wait_recv()
    fold_copies.wait_send()
    relay_copies = all_of(folded_in, folded_in, relay_send, relay_recv, N_WIN - 1)
    relay_copies.wait_send()
    relay_copies.wait_recv()
    own_band.wait()
    small_copies[4].wait()

    flat[...] = band_in[...].astype(F32).reshape(DEVICES * ROWS, 128)
    for r in range(ROWS):
        turned = flat[pl.ds(r, F, stride=ROWS), :].T
        at = (ROWS - 1 - r) * REACH
        lag_in[0, at : at + REACH, :] = turned[:REACH].astype(BF16)
        lag_in[1, at : at + REACH, :] = turned[REACH:].astype(BF16)
    flat_fold[...] = folded_in[...].astype(F32).reshape(DEVICES * 2, 128)
    for w in range(N_WIN):
        rows = flat_fold[pl.ds(2 * N_CHAN * w, N_CHAN, stride=2), :]
        by_bin[pl.ds(w, N_CHAN, stride=N_WIN), :] = rows
    turned_fold[...] = by_bin[...].T
    own = pl.multiple_of(win * ROWS, ROWS)
    pad = jnp.zeros((ROWS, F), F32)
    end = ROWS * REACH
    for part in range(2):
        mine = turned_fold[pl.ds(part * CH_DEV + own, ROWS), :]
        lag_in[part, end : end + 2 * ROWS, :] = jnp.concatenate([mine, pad], axis=0).astype(BF16)
    lagged = jnp.zeros((end + 2 * ROWS, NLAG), F32)
    for part in range(2):
        for half in range(2):
            lagged += jnp.dot(lag_in[part], inverse[2 * part + half], preferred_element_type=F32)
    near_ref[...] = lagged[:end].reshape(ROWS, REACH, NLAG)
    fold_ref[...] = lagged[end : end + ROWS]


def local(traces, quality, fold_block, fold_offset):
    vmem = pl.BlockSpec(memory_space=pltpu.VMEM)
    hbm = pl.BlockSpec(memory_space=pltpu.MemorySpace.HBM)
    phases, inverse = forward_phases(), inverse_halves()
    sem = pltpu.SemaphoreType.DMA
    near_lags, fold_lags = pl.pallas_call(
        kernel,
        out_shape=(
            jax.ShapeDtypeStruct((ROWS, REACH, NLAG), F32),
            jax.ShapeDtypeStruct((ROWS, NLAG), F32),
        ),
        in_specs=[hbm] * 6,
        out_specs=(vmem, vmem),
        scratch_shapes=[
            pltpu.VMEM((CHUNKS, LANES, L), BF16),
            pltpu.VMEM((1, CH_DEV), jnp.int32),
            pltpu.VMEM((1, CHANNELS), jnp.int32),
            pltpu.VMEM((1, CHANNELS), jnp.int32),
            pltpu.VMEM(phases.shape, F32),
            pltpu.VMEM(inverse.shape, BF16),
            pltpu.VMEM((2 * F, L), BF16),
            pltpu.VMEM((F + 16, LANES), F32),
            pltpu.VMEM((F * GROUP, 128), F32),
            pltpu.VMEM((DEVICES, CHUNKS, GROUP, 128), BF16),
            pltpu.VMEM((DEVICES, CHUNKS, GROUP, 128), BF16),
            pltpu.VMEM((2 * WINDOWS, CHANNELS + 128), BF16),
            pltpu.VMEM((CHANNELS, CHANNELS), BF16),
            pltpu.VMEM((DEVICES, ROWS, 128), BF16),
            pltpu.VMEM((N_CHAN, 2, 128), BF16),
            pltpu.VMEM((DEVICES, ROWS, 128), BF16),
            pltpu.VMEM((N_WIN, N_CHAN, 2, 128), BF16),
            pltpu.VMEM((DEVICES * ROWS, 128), F32),
            pltpu.VMEM((DEVICES * 2, 128), F32),
            pltpu.VMEM((F, 128), F32),
            pltpu.VMEM((2, ROWS * REACH + 2 * ROWS, F), BF16),
            pltpu.VMEM((128, F), F32),
            sem((CHUNKS,)),
            sem((5,)),
            sem((2,)),
            sem,
            sem((PAIRS,)),
            sem, sem, sem, sem, sem, sem,
        ],
        compiler_params=pltpu.CompilerParams(
            vmem_limit_bytes=60 << 20, collective_id=0, has_side_effects=True
        ),
    )(
        traces.reshape(WIN_DEV * CH_DEV, L),
        quality.reshape(1, CH_DEV),
        fold_block.reshape(1, CHANNELS),
        fold_offset.reshape(1, CHANNELS),
        phases,
        inverse,
    )
    factor = 1.0 / math.sqrt(F * WINDOWS)
    return near_lags * factor, fold_lags * factor


def solution(mesh):
    in_specs = (P("win", "chan", None), P("chan"), P(), P())
    out_specs = (P(("chan", "win"), None, None), P(("chan", "win"), None))
    return jax.shard_map(local, mesh=mesh, in_specs=in_specs, out_specs=out_specs, check_vma=False)
```

```python
import math

import jax
import jax.numpy as jnp
import ml_dtypes
import numpy as np
from jax import lax
from jax.experimental import pallas as pl
from jax.experimental.pallas import tpu as pltpu
from jax.sharding import PartitionSpec as P

F = 256
BAND_LO = 32
NLAG = 256
REACH = 64
L = 4096
CH_DEV = 64
CHANNELS = 2048
WINDOWS = 96
N_CHAN = 32
N_WIN = 8
DEVICES = N_CHAN * N_WIN
WIN_DEV = WINDOWS // N_WIN
ROWS = CHANNELS // DEVICES
SMOOTH = 4
STEP = 128
GROUP = 4
CHUNKS = WIN_DEV // GROUP
LANES = GROUP * CH_DEV
PAIR = 2 * N_WIN
PAIRS = DEVICES // PAIR
HALF = F // 2
GREETED = 13
MESH = pl.DeviceIdType.MESH
BF16 = jnp.bfloat16
F32 = jnp.float32


def forward_phases():
    bins = np.arange(F, dtype=np.int64).reshape(HALF, 2).T.reshape(F)
    frequency = bins[:, None] + BAND_LO
    fine = np.arange(STEP, dtype=np.int64)
    coarse = np.arange(L // 2 // STEP, dtype=np.int64) * STEP
    tables = []
    for steps in (fine, coarse):
        angles = (frequency * steps[None, :] % L).astype(np.float64) * (2.0 * math.pi / L)
        tables += [np.cos(angles), np.sin(angles)]
    joined = np.concatenate(tables, axis=1).astype(np.float32)
    return np.pad(joined, ((0, 0), (0, -joined.shape[1] % 128)))


def inverse_halves():
    shifts = np.arange(NLAG, dtype=np.int64)[None, :] + NLAG // 2
    frequency = np.arange(F, dtype=np.int64)[:, None] + BAND_LO
    angles = (frequency * shifts % NLAG).astype(np.float64) * (2.0 * math.pi / NLAG)
    halves = []
    for part in (np.cos(angles), -np.sin(angles)):
        high = part.astype(np.float32).astype(ml_dtypes.bfloat16)
        low = (part - high.astype(np.float64)).astype(np.float32).astype(ml_dtypes.bfloat16)
        halves += [high, low]
    return np.stack(halves)


def kernel(
    x_hbm, q_hbm, block_hbm, offset_hbm, phase_hbm, inverse_hbm, near_ref, fold_ref,
    xs, quality, fold_block, fold_offset, phase, inverse, table, energy, staged, sent, got, x, chosen,
    band, folded, band_in, folded_in, flat, flat_fold, by_bin, lag_in, turned_fold,
    x_sems, in_sems, own_sems, send_sem, recv_sems, band_send, band_recv, fold_send, fold_recv, relay_send, relay_recv,
):
    chan, win = lax.axis_index("chan"), lax.axis_index("win")
    me = chan * N_WIN + win

    wins = [lax.rem(win + k, N_WIN) for k in range(N_WIN)]
    side = lax.rem(chan, 2)
    sides = (side, 1 - side)
    neighbour = (lax.rem(chan + 1, N_CHAN), win)

    small_copies = [
        pltpu.make_async_copy(source, target, in_sems.at[i])
        for i, (source, target) in enumerate(
            [
                (phase_hbm, phase),
                (q_hbm, quality),
                (block_hbm, fold_block),
                (offset_hbm, fold_offset),
                (inverse_hbm, inverse),
            ]
        )
    ]
    x_copies = [
        pltpu.make_async_copy(x_hbm.at[pl.ds(i * LANES, LANES)], xs.at[i], x_sems.at[i])
        for i in range(CHUNKS)
    ]
    for copy in small_copies[:4] + x_copies + small_copies[4:]:
        copy.start()
    barrier = pltpu.get_barrier_semaphore()

    def greet(step, _):
        other = lax.rem(chan + step, N_CHAN)
        for k in range(N_WIN):
            pl.semaphore_signal(barrier, inc=1, device_id=(other, wins[k]), device_id_type=MESH)
        return 0

    for k in range(1, N_WIN):
        pl.semaphore_signal(barrier, inc=1, device_id=(chan, wins[k]), device_id_type=MESH)
    lax.fori_loop(1, GREETED, greet, 0)

    small_copies[0].wait()
    coarse_at = 2 * STEP
    blocks = L // 2 // STEP
    fine_cos, fine_sin = phase[:, 0:STEP], phase[:, STEP : 2 * STEP]
    for block in range(max(blocks, N_CHAN)):
        if GREETED <= block < N_CHAN:
            greet(block, 0)
        if block >= blocks:
            continue
        cos_b = phase[:, coarse_at + block : coarse_at + block + 1]
        sin_b = phase[:, coarse_at + blocks + block : coarse_at + blocks + block + 1]
        lanes = slice(block * STEP, (block + 1) * STEP)
        cosines = (fine_cos * cos_b - fine_sin * sin_b).astype(BF16)
        sines = (-fine_sin * cos_b - fine_cos * sin_b).astype(BF16)
        for odd in range(2):
            table[odd, 0:HALF, lanes] = cosines[odd * HALF : (odd + 1) * HALF]
            table[odd, HALF:F, lanes] = sines[odd * HALF : (odd + 1) * HALF]
    edge = jnp.zeros((8, LANES), F32)
    for odd in range(2):
        energy[odd, 0:8, :] = edge
        energy[odd, 8 + HALF : 16 + HALF, :] = edge

    for copy in small_copies[1:4]:
        copy.wait()
    low = lax.broadcasted_iota(jnp.int32, (HALF, 128), 1) < CH_DEV
    keep = jnp.concatenate([quality[...].astype(F32)] * GROUP, axis=1)
    over_lanes = (((1,), (1,)), ((), ()))
    for i in range(CHUNKS):
        x_copies[i].wait()
        early, late = xs[i, :, 0 : L // 2], xs[i, :, L // 2 : L]
        parts, powers = [], []
        for odd, mixed in enumerate((early + late, early - late)):
            spectra = lax.dot_general(table[odd], mixed, over_lanes, preferred_element_type=F32)
            re, im = spectra[0:HALF], spectra[HALF:F]
            power = re * re + im * im
            energy[odd, 8 : 8 + HALF, :] = power
            parts.append((re, im))
            powers.append(power)
        water = jnp.sum(powers[0] + powers[1], axis=0, keepdims=True) * (1.0 / F)
        for odd, (re, im) in enumerate(parts):
            near_bins = [(odd, d) for d in (-2, -1, 1, 2)]
            near_bins += [(1 - odd, d) for d in ((-1, 0, 1, 2) if odd else (-2, -1, 0, 1))]
            smooth = powers[odd]
            for which, d in near_bins:
                smooth = smooth + energy[which, 8 + d : 8 + d + HALF, :]
            scaling = lax.rsqrt(smooth * (1.0 / (2 * SMOOTH + 1)) + 0.1 * water + 1e-06) * keep
            re, im = re * scaling, im * scaling
            for half in range(GROUP // 2):
                re_p = re[:, half * 128 : half * 128 + 128]
                im_p = im[:, half * 128 : half * 128 + 128]
                first = jnp.where(low, re_p, pltpu.roll(im_p, CH_DEV, 1))
                second = jnp.where(low, pltpu.roll(re_p, CH_DEV, 1), im_p)
                at = GROUP * odd + 2 * half
                staged[pl.ds(at, HALF, stride=2 * GROUP), :] = first
                staged[pl.ds(at + 1, HALF, stride=2 * GROUP), :] = second
        sent[:, i] = staged[...].reshape(F, GROUP, 128).astype(BF16)

    pl.semaphore_wait(barrier, DEVICES - 1)

    pair = chan // 2
    own_copy = pltpu.make_async_copy(sent.at[me], got.at[me], recv_sems.at[pair])
    own_copy.start()

    def send_to(source, target, send, recv, m, own):
        for h in range(2):
            other = 2 * m + sides[h]
            for k in range(1 if own and h == 0 else 0, N_WIN):
                pltpu.make_async_remote_copy(
                    source.at[other * N_WIN + wins[k]], target.at[me], send, recv,
                    device_id=(other, wins[k]), device_id_type=MESH,
                ).start()

    def send_spectra(step, _):
        m = lax.rem(pair + step, PAIRS)
        send_to(sent, got, send_sem, recv_sems.at[pair], m, False)
        return 0

    send_to(sent, got, send_sem, recv_sems.at[pair], pair, True)
    lax.fori_loop(1, PAIRS, send_spectra, 0)

    wanted_all = fold_block[...] * CH_DEV + fold_offset[...]
    fold_offset[...] = wanted_all

    def choose(g, _):
        lanes = pl.ds(pl.multiple_of(g * 256, 256), 256)
        rows = lax.broadcasted_iota(jnp.int32, (CHANNELS, 256), 0)
        chosen[:, lanes] = jnp.where(rows == fold_offset[:, lanes], 1.0, 0.0).astype(BF16)
        return 0

    lax.fori_loop(0, CHANNELS // 256, choose, 0)
    x[:, CHANNELS : CHANNELS + 128] = jnp.zeros((2 * WINDOWS, 128), BF16)

    def all_of(source, target, send, recv, count):
        some = pl.ds(0, count)
        return pltpu.make_async_remote_copy(
            source.at[some], target.at[some], send, recv,
            device_id=neighbour, device_id_type=MESH,
        )

    low_w = lax.broadcasted_iota(jnp.int32, (WINDOWS, 128), 1) < CH_DEV
    low_out = lax.broadcasted_iota(jnp.int32, (128, 128), 1) < CH_DEV
    row_ids = lax.broadcasted_iota(jnp.int32, (128, 128), 0)
    lane_ids = lax.broadcasted_iota(jnp.int32, (128, 128), 1)
    mirror = jnp.where(row_ids + lane_ids == 127, 1.0, 0.0).astype(BF16)
    over_rows = (((0,), (0,)), ((), ()))

    def unpack(m):
        all_of(sent, got, send_sem, recv_sems.at[m], PAIR).wait_recv()
        even = got[pl.ds(PAIR * m, N_WIN)].astype(F32).reshape(WINDOWS, 128)
        odd = got[pl.ds(PAIR * m + N_WIN, N_WIN)].astype(F32).reshape(WINDOWS, 128)
        lanes = pl.ds(pl.multiple_of(m * 128, 128), 128)
        x[0:WINDOWS, lanes] = jnp.where(low_w, even, pltpu.roll(odd, CH_DEV, 1)).astype(BF16)
        x[WINDOWS : 2 * WINDOWS, lanes] = jnp.where(low_w, pltpu.roll(even, CH_DEV, 1), odd).astype(BF16)

    def near(m):
        right = x[:, pl.ds(pl.multiple_of(m * 128, 128), 256)]
        left = jnp.dot(right[:, :128], mirror, preferred_element_type=F32)
        turned = jnp.concatenate([left[WINDOWS:], -left[:WINDOWS]], axis=0).astype(BF16)
        left = left.astype(BF16)
        re = lax.dot_general(left, right, over_rows, preferred_element_type=F32)
        im = lax.dot_general(turned, right, over_rows, preferred_element_type=F32)
        re = pltpu.roll(re, 128, 1, stride=1, stride_axis=0)[:, :128]
        im = pltpu.roll(im, 192, 1, stride=1, stride_axis=0)[:, :128]
        both = jnp.where(low_out, re, im).astype(BF16)
        for g in range(PAIR):
            band[PAIR * m + PAIR - 1 - g] = both[g * ROWS : (g + 1) * ROWS]

    def send_band(m, own):
        send_to(band, band_in, band_send, band_recv, m, own)

    unpack(pair)

    def arrive(step, _):
        m = lax.rem(pair + PAIRS - step, PAIRS)
        unpack(m)
        near(m)
        send_band(m, False)
        return 0

    lax.fori_loop(1, PAIRS - 1, arrive, 0)
    last = lax.rem(pair + 1, PAIRS)
    unpack(last)

    low_1 = lax.broadcasted_iota(jnp.int32, (2, 128), 1) < CH_DEV

    def fold_group(g, _):
        lanes = pl.ds(pl.multiple_of(g * 256, 256), 256)
        partner = jnp.dot(x[:, 0:CHANNELS], chosen[:, lanes], preferred_element_type=F32)
        own = x[:, lanes].astype(F32)
        re_a, im_a = own[:WINDOWS], own[WINDOWS:]
        re_b, im_b = partner[:WINDOWS], partner[WINDOWS:]
        re_c = jnp.sum(re_a * re_b + im_a * im_b, axis=0, keepdims=True)
        im_c = jnp.sum(im_a * re_b - re_a * im_b, axis=0, keepdims=True)
        re_c = jnp.broadcast_to(re_c, (2, 256))
        im_c = jnp.broadcast_to(im_c, (2, 256))
        for half in range(2):
            re_p = re_c[:, half * 128 : half * 128 + 128]
            im_p = im_c[:, half * 128 : half * 128 + 128]
            even = jnp.where(low_1, re_p, pltpu.roll(im_p, CH_DEV, 1)).astype(BF16)
            odd = jnp.where(low_1, pltpu.roll(re_p, CH_DEV, 1), im_p).astype(BF16)
            folded[4 * g + 2 * half] = even
            folded[4 * g + 2 * half + 1] = odd
        return 0

    lax.fori_loop(0, CHANNELS // 256, fold_group, 0)

    own_fold = pltpu.make_async_copy(folded.at[chan], folded_in.at[win, chan], own_sems.at[0])
    own_fold.start()

    def send_fold(step, _):
        other = lax.rem(chan + step, N_CHAN)
        pltpu.make_async_remote_copy(
            folded.at[other], folded_in.at[win, chan], fold_send, fold_recv,
            device_id=(other, win), device_id_type=MESH,
        ).start()
        return 0

    lax.fori_loop(1, N_CHAN, send_fold, 0)

    near(last)
    send_band(last, False)
    near(pair)
    own_band = pltpu.make_async_copy(band.at[me], band_in.at[me], own_sems.at[1])
    own_band.start()
    send_band(pair, True)

    own_fold.wait()
    fold_copies = all_of(folded, folded, fold_send, fold_recv, N_CHAN - 1)
    fold_copies.wait_recv()

    def relay(step, _):
        pltpu.make_async_remote_copy(
            folded_in.at[win], folded_in.at[win], relay_send, relay_recv,
            device_id=(chan, lax.rem(win + step, N_WIN)), device_id_type=MESH,
        ).start()
        return 0

    lax.fori_loop(1, N_WIN, relay, 0)

    all_of(sent, got, send_sem, recv_sems.at[0], DEVICES - 1).wait_send()
    band_copies = all_of(band, band_in, band_send, band_recv, DEVICES - 1)
    band_copies.wait_send()
    band_copies.wait_recv()
    fold_copies.wait_send()
    relay_copies = all_of(folded_in, folded_in, relay_send, relay_recv, N_WIN - 1)
    relay_copies.wait_send()
    relay_copies.wait_recv()
    own_band.wait()
    small_copies[4].wait()

    flat[...] = band_in[...].astype(F32).reshape(DEVICES * ROWS, 128)
    for r in range(ROWS):
        turned = flat[pl.ds(r, F, stride=ROWS), :].T
        at = (ROWS - 1 - r) * REACH
        lag_in[0, at : at + REACH, :] = turned[:REACH].astype(BF16)
        lag_in[1, at : at + REACH, :] = turned[REACH:].astype(BF16)
    flat_fold[...] = folded_in[...].astype(F32).reshape(DEVICES * 2, 128)
    for w in range(N_WIN):
        rows = flat_fold[pl.ds(2 * N_CHAN * w, N_CHAN, stride=2), :]
        by_bin[pl.ds(w, N_CHAN, stride=N_WIN), :] = rows
    turned_fold[...] = by_bin[...].T
    own = pl.multiple_of(win * ROWS, ROWS)
    pad = jnp.zeros((ROWS, F), F32)
    end = ROWS * REACH
    for part in range(2):
        mine = turned_fold[pl.ds(part * CH_DEV + own, ROWS), :]
        lag_in[part, end : end + 2 * ROWS, :] = jnp.concatenate([mine, pad], axis=0).astype(BF16)
    lagged = jnp.zeros((end + 2 * ROWS, NLAG), F32)
    for part in range(2):
        for half in range(2):
            lagged += jnp.dot(lag_in[part], inverse[2 * part + half], preferred_element_type=F32)
    near_ref[...] = lagged[:end].reshape(ROWS, REACH, NLAG)
    fold_ref[...] = lagged[end : end + ROWS]


def hand_over(near_in, fold_in, near_out, fold_out):
    factor = 1.0 / math.sqrt(F * WINDOWS)
    near_out[...] = near_in[...] * factor
    fold_out[...] = fold_in[...] * factor


def local(traces, quality, fold_block, fold_offset):
    vmem = pl.BlockSpec(memory_space=pltpu.VMEM)
    hbm = pl.BlockSpec(memory_space=pltpu.MemorySpace.HBM)
    phases, inverse = forward_phases(), inverse_halves()
    sem = pltpu.SemaphoreType.DMA
    near_lags, fold_lags = pl.pallas_call(
        kernel,
        out_shape=(
            jax.ShapeDtypeStruct((ROWS, REACH, NLAG), F32),
            jax.ShapeDtypeStruct((ROWS, NLAG), F32),
        ),
        in_specs=[hbm] * 6,
        out_specs=(vmem, vmem),
        scratch_shapes=[
            pltpu.VMEM((CHUNKS, LANES, L), BF16),
            pltpu.VMEM((1, CH_DEV), jnp.int32),
            pltpu.VMEM((1, CHANNELS), jnp.int32),
            pltpu.VMEM((1, CHANNELS), jnp.int32),
            pltpu.VMEM(phases.shape, F32),
            pltpu.VMEM(inverse.shape, BF16),
            pltpu.VMEM((2, F, L // 2), BF16),
            pltpu.VMEM((2, HALF + 16, LANES), F32),
            pltpu.VMEM((F * GROUP, 128), F32),
            pltpu.VMEM((DEVICES, CHUNKS, GROUP, 128), BF16),
            pltpu.VMEM((DEVICES, CHUNKS, GROUP, 128), BF16),
            pltpu.VMEM((2 * WINDOWS, CHANNELS + 128), BF16),
            pltpu.VMEM((CHANNELS, CHANNELS), BF16),
            pltpu.VMEM((DEVICES, ROWS, 128), BF16),
            pltpu.VMEM((N_CHAN, 2, 128), BF16),
            pltpu.VMEM((DEVICES, ROWS, 128), BF16),
            pltpu.VMEM((N_WIN, N_CHAN, 2, 128), BF16),
            pltpu.VMEM((DEVICES * ROWS, 128), F32),
            pltpu.VMEM((DEVICES * 2, 128), F32),
            pltpu.VMEM((F, 128), F32),
            pltpu.VMEM((2, ROWS * REACH + 2 * ROWS, F), BF16),
            pltpu.VMEM((128, F), F32),
            sem((CHUNKS,)),
            sem((5,)),
            sem((2,)),
            sem,
            sem((PAIRS,)),
            sem, sem, sem, sem, sem, sem,
        ],
        compiler_params=pltpu.CompilerParams(
            vmem_limit_bytes=60 << 20, collective_id=0, has_side_effects=True
        ),
    )(
        traces.reshape(WIN_DEV * CH_DEV, L),
        quality.reshape(1, CH_DEV),
        fold_block.reshape(1, CHANNELS),
        fold_offset.reshape(1, CHANNELS),
        phases,
        inverse,
    )
    shapes = tuple(jax.ShapeDtypeStruct(a.shape, a.dtype) for a in (near_lags, fold_lags))
    return pl.pallas_call(
        hand_over,
        grid=(2,),
        out_shape=shapes,
        in_specs=[
            pl.BlockSpec((ROWS // 2, REACH, NLAG), lambda i: (i, 0, 0)),
            pl.BlockSpec((ROWS, NLAG), lambda i: (0, 0)),
        ],
        out_specs=(
            pl.BlockSpec((ROWS // 2, REACH, NLAG), lambda i: (i, 0, 0)),
            pl.BlockSpec((ROWS, NLAG), lambda i: (0, 0)),
        ),
        compiler_params=pltpu.CompilerParams(vmem_limit_bytes=60 << 20),
    )(near_lags, fold_lags)


def solution(mesh):
    in_specs = (P("win", "chan", None), P("chan"), P(), P())
    out_specs = (P(("chan", "win"), None, None), P(("chan", "win"), None))
    return jax.shard_map(local, mesh=mesh, in_specs=in_specs, out_specs=out_specs, check_vma=False)
```

```python
import math

import jax
import jax.numpy as jnp
import ml_dtypes
import numpy as np
from jax import lax
from jax.experimental import pallas as pl
from jax.experimental.pallas import tpu as pltpu
from jax.sharding import PartitionSpec as P

F = 256
BAND_LO = 32
NLAG = 256
REACH = 64
L = 4096
CH_DEV = 64
CHANNELS = 2048
WINDOWS = 96
N_CHAN = 32
N_WIN = 8
DEVICES = N_CHAN * N_WIN
WIN_DEV = WINDOWS // N_WIN
ROWS = CHANNELS // DEVICES
SMOOTH = 4
STEP = 128
GROUP = 4
CHUNKS = WIN_DEV // GROUP
LANES = GROUP * CH_DEV
PAIR = 2 * N_WIN
PAIRS = DEVICES // PAIR
HALF = F // 2
GREETED = 13
MESH = pl.DeviceIdType.MESH
BF16 = jnp.bfloat16
F32 = jnp.float32


def forward_phases():
    bins = np.arange(F, dtype=np.int64).reshape(HALF, 2).T.reshape(F)
    frequency = bins[:, None] + BAND_LO
    fine = np.arange(STEP, dtype=np.int64)
    coarse = np.arange(L // 2 // STEP, dtype=np.int64) * STEP
    tables = []
    for steps in (fine, coarse):
        angles = (frequency * steps[None, :] % L).astype(np.float64) * (2.0 * math.pi / L)
        tables += [np.cos(angles), np.sin(angles)]
    joined = np.concatenate(tables, axis=1).astype(np.float32)
    return np.pad(joined, ((0, 0), (0, -joined.shape[1] % 128)))


def inverse_halves():
    shifts = np.arange(NLAG, dtype=np.int64)[None, :] + NLAG // 2
    frequency = np.arange(F, dtype=np.int64)[:, None] + BAND_LO
    angles = (frequency * shifts % NLAG).astype(np.float64) * (2.0 * math.pi / NLAG)
    halves = []
    for part in (np.cos(angles), -np.sin(angles)):
        high = part.astype(np.float32).astype(ml_dtypes.bfloat16)
        low = (part - high.astype(np.float64)).astype(np.float32).astype(ml_dtypes.bfloat16)
        halves += [high, low]
    return np.stack(halves)


def kernel(
    x_hbm, q_hbm, block_hbm, offset_hbm, phase_hbm, inverse_hbm, near_ref, fold_ref,
    xs, quality, fold_block, fold_offset, phase, inverse, table, energy, staged, sent, got, x, chosen,
    band, folded, band_in, folded_in, flat, flat_fold, by_bin, lag_in, turned_fold,
    x_sems, in_sems, own_sems, send_sem, recv_sems, band_send, band_recv, fold_send, fold_recv, relay_send, relay_recv,
):
    chan, win = lax.axis_index("chan"), lax.axis_index("win")
    me = chan * N_WIN + win

    wins = [lax.rem(win + k, N_WIN) for k in range(N_WIN)]
    side = lax.rem(chan, 2)
    sides = (side, 1 - side)
    neighbour = (lax.rem(chan + 1, N_CHAN), win)

    small_copies = [
        pltpu.make_async_copy(source, target, in_sems.at[i])
        for i, (source, target) in enumerate(
            [
                (phase_hbm, phase),
                (q_hbm, quality),
                (block_hbm, fold_block),
                (offset_hbm, fold_offset),
                (inverse_hbm, inverse),
            ]
        )
    ]
    x_copies = [
        pltpu.make_async_copy(x_hbm.at[pl.ds(i * LANES, LANES)], xs.at[i], x_sems.at[i])
        for i in range(CHUNKS)
    ]
    for copy in small_copies[:4] + x_copies + small_copies[4:]:
        copy.start()
    barrier = pltpu.get_barrier_semaphore()

    def greet(step, _):
        other = lax.rem(chan + step, N_CHAN)
        for k in range(N_WIN):
            pl.semaphore_signal(barrier, inc=1, device_id=(other, wins[k]), device_id_type=MESH)
        return 0

    for k in range(1, N_WIN):
        pl.semaphore_signal(barrier, inc=1, device_id=(chan, wins[k]), device_id_type=MESH)
    lax.fori_loop(1, GREETED, greet, 0)

    small_copies[0].wait()
    coarse_at = 2 * STEP
    blocks = L // 2 // STEP
    fine_cos, fine_sin = phase[:, 0:STEP], phase[:, STEP : 2 * STEP]
    for block in range(max(blocks, N_CHAN)):
        if GREETED <= block < N_CHAN:
            greet(block, 0)
        if block >= blocks:
            continue
        cos_b = phase[:, coarse_at + block : coarse_at + block + 1]
        sin_b = phase[:, coarse_at + blocks + block : coarse_at + blocks + block + 1]
        lanes = slice(block * STEP, (block + 1) * STEP)
        cosines = (fine_cos * cos_b - fine_sin * sin_b).astype(BF16)
        sines = (-fine_sin * cos_b - fine_cos * sin_b).astype(BF16)
        for odd in range(2):
            later = slice(L // 2 + block * STEP, L // 2 + (block + 1) * STEP)
            for row, part in ((0, cosines), (HALF, sines)):
                part = part[odd * HALF : (odd + 1) * HALF]
                table[odd, row : row + HALF, lanes] = part
                table[odd, row : row + HALF, later] = -part if odd else part
    edge = jnp.zeros((8, LANES), F32)
    for odd in range(2):
        energy[odd, 0:8, :] = edge
        energy[odd, 8 + HALF : 16 + HALF, :] = edge

    for copy in small_copies[1:4]:
        copy.wait()
    low = lax.broadcasted_iota(jnp.int32, (HALF, 128), 1) < CH_DEV
    keep = jnp.concatenate([quality[...].astype(F32)] * GROUP, axis=1)
    over_lanes = (((1,), (1,)), ((), ()))
    for i in range(CHUNKS):
        x_copies[i].wait()
        parts, powers = [], []
        for odd in range(2):
            spectra = lax.dot_general(table[odd], xs[i], over_lanes, preferred_element_type=F32)
            re, im = spectra[0:HALF], spectra[HALF:F]
            power = re * re + im * im
            energy[odd, 8 : 8 + HALF, :] = power
            parts.append((re, im))
            powers.append(power)
        water = jnp.sum(powers[0] + powers[1], axis=0, keepdims=True) * (1.0 / F)
        for odd, (re, im) in enumerate(parts):
            near_bins = [(odd, d) for d in (-2, -1, 1, 2)]
            near_bins += [(1 - odd, d) for d in ((-1, 0, 1, 2) if odd else (-2, -1, 0, 1))]
            smooth = powers[odd]
            for which, d in near_bins:
                smooth = smooth + energy[which, 8 + d : 8 + d + HALF, :]
            scaling = lax.rsqrt(smooth * (1.0 / (2 * SMOOTH + 1)) + 0.1 * water + 1e-06) * keep
            re, im = re * scaling, im * scaling
            for half in range(GROUP // 2):
                re_p = re[:, half * 128 : half * 128 + 128]
                im_p = im[:, half * 128 : half * 128 + 128]
                first = jnp.where(low, re_p, pltpu.roll(im_p, CH_DEV, 1))
                second = jnp.where(low, pltpu.roll(re_p, CH_DEV, 1), im_p)
                at = GROUP * odd + 2 * half
                staged[pl.ds(at, HALF, stride=2 * GROUP), :] = first
                staged[pl.ds(at + 1, HALF, stride=2 * GROUP), :] = second
        sent[:, i] = staged[...].reshape(F, GROUP, 128).astype(BF16)

    pl.semaphore_wait(barrier, DEVICES - 1)

    pair = chan // 2
    own_copy = pltpu.make_async_copy(sent.at[me], got.at[me], recv_sems.at[pair])
    own_copy.start()

    def send_to(source, target, send, recv, m, own):
        for h in range(2):
            other = 2 * m + sides[h]
            for k in range(1 if own and h == 0 else 0, N_WIN):
                pltpu.make_async_remote_copy(
                    source.at[other * N_WIN + wins[k]], target.at[me], send, recv,
                    device_id=(other, wins[k]), device_id_type=MESH,
                ).start()

    def send_spectra(step, _):
        m = lax.rem(pair + step, PAIRS)
        send_to(sent, got, send_sem, recv_sems.at[pair], m, False)
        return 0

    send_to(sent, got, send_sem, recv_sems.at[pair], pair, True)
    lax.fori_loop(1, PAIRS, send_spectra, 0)

    wanted_all = fold_block[...] * CH_DEV + fold_offset[...]
    fold_offset[...] = wanted_all

    def choose(g, _):
        lanes = pl.ds(pl.multiple_of(g * 256, 256), 256)
        rows = lax.broadcasted_iota(jnp.int32, (CHANNELS, 256), 0)
        chosen[:, lanes] = jnp.where(rows == fold_offset[:, lanes], 1.0, 0.0).astype(BF16)
        return 0

    lax.fori_loop(0, CHANNELS // 256, choose, 0)
    x[:, CHANNELS : CHANNELS + 128] = jnp.zeros((2 * WINDOWS, 128), BF16)

    def all_of(source, target, send, recv, count):
        some = pl.ds(0, count)
        return pltpu.make_async_remote_copy(
            source.at[some], target.at[some], send, recv,
            device_id=neighbour, device_id_type=MESH,
        )

    low_w = lax.broadcasted_iota(jnp.int32, (WINDOWS, 128), 1) < CH_DEV
    low_out = lax.broadcasted_iota(jnp.int32, (128, 128), 1) < CH_DEV
    row_ids = lax.broadcasted_iota(jnp.int32, (128, 128), 0)
    lane_ids = lax.broadcasted_iota(jnp.int32, (128, 128), 1)
    mirror = jnp.where(row_ids + lane_ids == 127, 1.0, 0.0).astype(BF16)
    over_rows = (((0,), (0,)), ((), ()))

    def unpack(m):
        all_of(sent, got, send_sem, recv_sems.at[m], PAIR).wait_recv()
        even = got[pl.ds(PAIR * m, N_WIN)].astype(F32).reshape(WINDOWS, 128)
        odd = got[pl.ds(PAIR * m + N_WIN, N_WIN)].astype(F32).reshape(WINDOWS, 128)
        lanes = pl.ds(pl.multiple_of(m * 128, 128), 128)
        x[0:WINDOWS, lanes] = jnp.where(low_w, even, pltpu.roll(odd, CH_DEV, 1)).astype(BF16)
        x[WINDOWS : 2 * WINDOWS, lanes] = jnp.where(low_w, pltpu.roll(even, CH_DEV, 1), odd).astype(BF16)

    def near(m):
        right = x[:, pl.ds(pl.multiple_of(m * 128, 128), 256)]
        left = jnp.dot(right[:, :128], mirror, preferred_element_type=F32)
        turned = jnp.concatenate([left[WINDOWS:], -left[:WINDOWS]], axis=0).astype(BF16)
        left = left.astype(BF16)
        re = lax.dot_general(left, right, over_rows, preferred_element_type=F32)
        im = lax.dot_general(turned, right, over_rows, preferred_element_type=F32)
        re = pltpu.roll(re, 128, 1, stride=1, stride_axis=0)[:, :128]
        im = pltpu.roll(im, 192, 1, stride=1, stride_axis=0)[:, :128]
        both = jnp.where(low_out, re, im).astype(BF16)
        for g in range(PAIR):
            band[PAIR * m + PAIR - 1 - g] = both[g * ROWS : (g + 1) * ROWS]

    def send_band(m, own):
        send_to(band, band_in, band_send, band_recv, m, own)

    unpack(pair)

    def arrive(step, _):
        m = lax.rem(pair + PAIRS - step, PAIRS)
        unpack(m)
        near(m)
        send_band(m, False)
        return 0

    lax.fori_loop(1, PAIRS - 1, arrive, 0)
    last = lax.rem(pair + 1, PAIRS)
    unpack(last)

    low_1 = lax.broadcasted_iota(jnp.int32, (2, 128), 1) < CH_DEV

    def fold_group(g, _):
        lanes = pl.ds(pl.multiple_of(g * 256, 256), 256)
        partner = jnp.dot(x[:, 0:CHANNELS], chosen[:, lanes], preferred_element_type=F32)
        own = x[:, lanes].astype(F32)
        re_a, im_a = own[:WINDOWS], own[WINDOWS:]
        re_b, im_b = partner[:WINDOWS], partner[WINDOWS:]
        re_c = jnp.sum(re_a * re_b + im_a * im_b, axis=0, keepdims=True)
        im_c = jnp.sum(im_a * re_b - re_a * im_b, axis=0, keepdims=True)
        re_c = jnp.broadcast_to(re_c, (2, 256))
        im_c = jnp.broadcast_to(im_c, (2, 256))
        for half in range(2):
            re_p = re_c[:, half * 128 : half * 128 + 128]
            im_p = im_c[:, half * 128 : half * 128 + 128]
            even = jnp.where(low_1, re_p, pltpu.roll(im_p, CH_DEV, 1)).astype(BF16)
            odd = jnp.where(low_1, pltpu.roll(re_p, CH_DEV, 1), im_p).astype(BF16)
            folded[4 * g + 2 * half] = even
            folded[4 * g + 2 * half + 1] = odd
        return 0

    lax.fori_loop(0, CHANNELS // 256, fold_group, 0)

    own_fold = pltpu.make_async_copy(folded.at[chan], folded_in.at[win, chan], own_sems.at[0])
    own_fold.start()

    def send_fold(step, _):
        other = lax.rem(chan + step, N_CHAN)
        pltpu.make_async_remote_copy(
            folded.at[other], folded_in.at[win, chan], fold_send, fold_recv,
            device_id=(other, win), device_id_type=MESH,
        ).start()
        return 0

    lax.fori_loop(1, N_CHAN, send_fold, 0)

    near(last)
    send_band(last, False)
    near(pair)
    own_band = pltpu.make_async_copy(band.at[me], band_in.at[me], own_sems.at[1])
    own_band.start()
    send_band(pair, True)

    own_fold.wait()
    fold_copies = all_of(folded, folded, fold_send, fold_recv, N_CHAN - 1)
    fold_copies.wait_recv()

    def relay(step, _):
        pltpu.make_async_remote_copy(
            folded_in.at[win], folded_in.at[win], relay_send, relay_recv,
            device_id=(chan, lax.rem(win + step, N_WIN)), device_id_type=MESH,
        ).start()
        return 0

    lax.fori_loop(1, N_WIN, relay, 0)

    all_of(sent, got, send_sem, recv_sems.at[0], DEVICES - 1).wait_send()
    band_copies = all_of(band, band_in, band_send, band_recv, DEVICES - 1)
    band_copies.wait_send()
    band_copies.wait_recv()
    fold_copies.wait_send()
    relay_copies = all_of(folded_in, folded_in, relay_send, relay_recv, N_WIN - 1)
    relay_copies.wait_send()
    relay_copies.wait_recv()
    own_band.wait()
    small_copies[4].wait()

    flat[...] = band_in[...].astype(F32).reshape(DEVICES * ROWS, 128)
    for r in range(ROWS):
        turned = flat[pl.ds(r, F, stride=ROWS), :].T
        at = (ROWS - 1 - r) * REACH
        lag_in[0, at : at + REACH, :] = turned[:REACH].astype(BF16)
        lag_in[1, at : at + REACH, :] = turned[REACH:].astype(BF16)
    flat_fold[...] = folded_in[...].astype(F32).reshape(DEVICES * 2, 128)
    for w in range(N_WIN):
        rows = flat_fold[pl.ds(2 * N_CHAN * w, N_CHAN, stride=2), :]
        by_bin[pl.ds(w, N_CHAN, stride=N_WIN), :] = rows
    turned_fold[...] = by_bin[...].T
    own = pl.multiple_of(win * ROWS, ROWS)
    pad = jnp.zeros((ROWS, F), F32)
    end = ROWS * REACH
    for part in range(2):
        mine = turned_fold[pl.ds(part * CH_DEV + own, ROWS), :]
        lag_in[part, end : end + 2 * ROWS, :] = jnp.concatenate([mine, pad], axis=0).astype(BF16)
    lagged = jnp.zeros((end + 2 * ROWS, NLAG), F32)
    for part in range(2):
        for half in range(2):
            lagged += jnp.dot(lag_in[part], inverse[2 * part + half], preferred_element_type=F32)
    near_ref[...] = lagged[:end].reshape(ROWS, REACH, NLAG)
    fold_ref[...] = lagged[end : end + ROWS]


def hand_over(near_in, fold_in, near_out, fold_out):
    factor = 1.0 / math.sqrt(F * WINDOWS)
    near_out[...] = near_in[...] * factor
    fold_out[...] = fold_in[...] * factor


def local(traces, quality, fold_block, fold_offset):
    vmem = pl.BlockSpec(memory_space=pltpu.VMEM)
    hbm = pl.BlockSpec(memory_space=pltpu.MemorySpace.HBM)
    phases, inverse = forward_phases(), inverse_halves()
    sem = pltpu.SemaphoreType.DMA
    near_lags, fold_lags = pl.pallas_call(
        kernel,
        out_shape=(
            jax.ShapeDtypeStruct((ROWS, REACH, NLAG), F32),
            jax.ShapeDtypeStruct((ROWS, NLAG), F32),
        ),
        in_specs=[hbm] * 6,
        out_specs=(vmem, vmem),
        scratch_shapes=[
            pltpu.VMEM((CHUNKS, LANES, L), BF16),
            pltpu.VMEM((1, CH_DEV), jnp.int32),
            pltpu.VMEM((1, CHANNELS), jnp.int32),
            pltpu.VMEM((1, CHANNELS), jnp.int32),
            pltpu.VMEM(phases.shape, F32),
            pltpu.VMEM(inverse.shape, BF16),
            pltpu.VMEM((2, F, L), BF16),
            pltpu.VMEM((2, HALF + 16, LANES), F32),
            pltpu.VMEM((F * GROUP, 128), F32),
            pltpu.VMEM((DEVICES, CHUNKS, GROUP, 128), BF16),
            pltpu.VMEM((DEVICES, CHUNKS, GROUP, 128), BF16),
            pltpu.VMEM((2 * WINDOWS, CHANNELS + 128), BF16),
            pltpu.VMEM((CHANNELS, CHANNELS), BF16),
            pltpu.VMEM((DEVICES, ROWS, 128), BF16),
            pltpu.VMEM((N_CHAN, 2, 128), BF16),
            pltpu.VMEM((DEVICES, ROWS, 128), BF16),
            pltpu.VMEM((N_WIN, N_CHAN, 2, 128), BF16),
            pltpu.VMEM((DEVICES * ROWS, 128), F32),
            pltpu.VMEM((DEVICES * 2, 128), F32),
            pltpu.VMEM((F, 128), F32),
            pltpu.VMEM((2, ROWS * REACH + 2 * ROWS, F), BF16),
            pltpu.VMEM((128, F), F32),
            sem((CHUNKS,)),
            sem((5,)),
            sem((2,)),
            sem,
            sem((PAIRS,)),
            sem, sem, sem, sem, sem, sem,
        ],
        compiler_params=pltpu.CompilerParams(
            vmem_limit_bytes=60 << 20, collective_id=0, has_side_effects=True
        ),
    )(
        traces.reshape(WIN_DEV * CH_DEV, L),
        quality.reshape(1, CH_DEV),
        fold_block.reshape(1, CHANNELS),
        fold_offset.reshape(1, CHANNELS),
        phases,
        inverse,
    )
    shapes = tuple(jax.ShapeDtypeStruct(a.shape, a.dtype) for a in (near_lags, fold_lags))
    return pl.pallas_call(
        hand_over,
        grid=(2,),
        out_shape=shapes,
        in_specs=[
            pl.BlockSpec((ROWS // 2, REACH, NLAG), lambda i: (i, 0, 0)),
            pl.BlockSpec((ROWS, NLAG), lambda i: (0, 0)),
        ],
        out_specs=(
            pl.BlockSpec((ROWS // 2, REACH, NLAG), lambda i: (i, 0, 0)),
            pl.BlockSpec((ROWS, NLAG), lambda i: (0, 0)),
        ),
        compiler_params=pltpu.CompilerParams(vmem_limit_bytes=60 << 20),
    )(near_lags, fold_lags)


def solution(mesh):
    in_specs = (P("win", "chan", None), P("chan"), P(), P())
    out_specs = (P(("chan", "win"), None, None), P(("chan", "win"), None))
    return jax.shard_map(local, mesh=mesh, in_specs=in_specs, out_specs=out_specs, check_vma=False)
```

```python
import math

import jax
import jax.numpy as jnp
import ml_dtypes
import numpy as np
from jax import lax
from jax.experimental import pallas as pl
from jax.experimental.pallas import tpu as pltpu
from jax.sharding import PartitionSpec as P

F = 256
BAND_LO = 32
NLAG = 256
REACH = 64
L = 4096
CH_DEV = 64
CHANNELS = 2048
WINDOWS = 96
N_CHAN = 32
N_WIN = 8
DEVICES = N_CHAN * N_WIN
WIN_DEV = WINDOWS // N_WIN
ROWS = CHANNELS // DEVICES
SMOOTH = 4
STEP = 128
GROUP = 4
CHUNKS = WIN_DEV // GROUP
LANES = GROUP * CH_DEV
PAIR = 2 * N_WIN
PAIRS = DEVICES // PAIR
HALF = F // 2
GREETED = 13
MESH = pl.DeviceIdType.MESH
BF16 = jnp.bfloat16
F32 = jnp.float32


def forward_phases():
    bins = np.arange(F, dtype=np.int64).reshape(HALF, 2).T.reshape(F)
    frequency = bins[:, None] + BAND_LO
    fine = np.arange(STEP, dtype=np.int64)
    coarse = np.arange(L // 2 // STEP, dtype=np.int64) * STEP
    tables = []
    for steps in (fine, coarse):
        angles = (frequency * steps[None, :] % L).astype(np.float64) * (2.0 * math.pi / L)
        tables += [np.cos(angles), np.sin(angles)]
    joined = np.concatenate(tables, axis=1).astype(np.float32)
    return np.pad(joined, ((0, 0), (0, -joined.shape[1] % 128)))


def inverse_halves():
    shifts = np.arange(NLAG, dtype=np.int64)[None, :] + NLAG // 2
    frequency = np.arange(F, dtype=np.int64)[:, None] + BAND_LO
    angles = (frequency * shifts % NLAG).astype(np.float64) * (2.0 * math.pi / NLAG)
    halves = []
    for part in (np.cos(angles), -np.sin(angles)):
        high = part.astype(np.float32).astype(ml_dtypes.bfloat16)
        low = (part - high.astype(np.float64)).astype(np.float32).astype(ml_dtypes.bfloat16)
        halves += [high, low]
    return np.stack(halves)


def kernel(
    x_hbm, q_hbm, block_hbm, offset_hbm, phase_hbm, inverse_hbm, near_ref, fold_ref,
    xs, quality, fold_block, fold_offset, phase, inverse, table, energy, staged, sent, got, x, chosen,
    band, folded, band_in, folded_in, flat, flat_fold, by_bin, lag_in, turned_fold,
    x_sems, in_sems, own_sems, send_sem, recv_sems, band_send, band_recv, fold_send, fold_recv, relay_send, relay_recv,
):
    chan, win = lax.axis_index("chan"), lax.axis_index("win")
    me = chan * N_WIN + win

    wins = [lax.rem(win + k, N_WIN) for k in range(N_WIN)]
    side = lax.rem(chan, 2)
    sides = (side, 1 - side)
    neighbour = (lax.rem(chan + 1, N_CHAN), win)

    small_copies = [
        pltpu.make_async_copy(source, target, in_sems.at[i])
        for i, (source, target) in enumerate(
            [
                (phase_hbm, phase),
                (q_hbm, quality),
                (block_hbm, fold_block),
                (offset_hbm, fold_offset),
                (inverse_hbm, inverse),
            ]
        )
    ]
    x_copies = [
        pltpu.make_async_copy(x_hbm.at[pl.ds(i * LANES, LANES)], xs.at[i], x_sems.at[i])
        for i in range(CHUNKS)
    ]
    for copy in small_copies[:4] + x_copies + small_copies[4:]:
        copy.start()
    barrier = pltpu.get_barrier_semaphore()

    def greet(step, _):
        other = lax.rem(chan + step, N_CHAN)
        for k in range(N_WIN):
            pl.semaphore_signal(barrier, inc=1, device_id=(other, wins[k]), device_id_type=MESH)
        return 0

    for k in range(1, N_WIN):
        pl.semaphore_signal(barrier, inc=1, device_id=(chan, wins[k]), device_id_type=MESH)
    lax.fori_loop(1, GREETED, greet, 0)

    small_copies[0].wait()
    coarse_at = 2 * STEP
    blocks = L // 2 // STEP
    fine_cos, fine_sin = phase[:, 0:STEP], phase[:, STEP : 2 * STEP]
    for block in range(max(blocks, N_CHAN)):
        if GREETED <= block < N_CHAN:
            greet(block, 0)
        if block >= blocks:
            continue
        cos_b = phase[:, coarse_at + block : coarse_at + block + 1]
        sin_b = phase[:, coarse_at + blocks + block : coarse_at + blocks + block + 1]
        lanes = slice(block * STEP, (block + 1) * STEP)
        cosines = (fine_cos * cos_b - fine_sin * sin_b).astype(BF16)
        sines = (-fine_sin * cos_b - fine_cos * sin_b).astype(BF16)
        for odd in range(2):
            later = slice(L // 2 + block * STEP, L // 2 + (block + 1) * STEP)
            for row, part in ((0, cosines), (HALF, sines)):
                part = part[odd * HALF : (odd + 1) * HALF]
                table[odd, row : row + HALF, lanes] = part
                table[odd, row : row + HALF, later] = -part if odd else part
    edge = jnp.zeros((8, LANES), F32)
    for odd in range(2):
        energy[odd, 0:8, :] = edge
        energy[odd, 8 + HALF : 16 + HALF, :] = edge

    for copy in small_copies[1:4]:
        copy.wait()
    low = lax.broadcasted_iota(jnp.int32, (HALF, 128), 1) < CH_DEV
    keep = jnp.concatenate([quality[...].astype(F32)] * GROUP, axis=1)
    over_lanes = (((1,), (1,)), ((), ()))
    for i in range(CHUNKS):
        x_copies[i].wait()
        parts, powers = [], []
        for odd in range(2):
            spectra = lax.dot_general(table[odd], xs[i], over_lanes, preferred_element_type=F32)
            re, im = spectra[0:HALF], spectra[HALF:F]
            power = re * re + im * im
            energy[odd, 8 : 8 + HALF, :] = power
            parts.append((re, im))
            powers.append(power)
        water = jnp.sum(powers[0] + powers[1], axis=0, keepdims=True) * (1.0 / F)
        for odd, (re, im) in enumerate(parts):
            near_bins = [(odd, d) for d in (-2, -1, 1, 2)]
            near_bins += [(1 - odd, d) for d in ((-1, 0, 1, 2) if odd else (-2, -1, 0, 1))]
            smooth = powers[odd]
            for which, d in near_bins:
                smooth = smooth + energy[which, 8 + d : 8 + d + HALF, :]
            scaling = lax.rsqrt(smooth * (1.0 / (2 * SMOOTH + 1)) + 0.1 * water + 1e-06) * keep
            re, im = re * scaling, im * scaling
            for half in range(GROUP // 2):
                re_p = re[:, half * 128 : half * 128 + 128]
                im_p = im[:, half * 128 : half * 128 + 128]
                first = jnp.where(low, re_p, pltpu.roll(im_p, CH_DEV, 1))
                second = jnp.where(low, pltpu.roll(re_p, CH_DEV, 1), im_p)
                at = GROUP * odd + 2 * half
                staged[pl.ds(at, HALF, stride=2 * GROUP), :] = first
                staged[pl.ds(at + 1, HALF, stride=2 * GROUP), :] = second
        sent[:, i] = staged[...].reshape(F, GROUP, 128).astype(BF16)

    pl.semaphore_wait(barrier, DEVICES - 1)

    pair = chan // 2
    own_copy = pltpu.make_async_copy(sent.at[me], got.at[me], recv_sems.at[pair])
    own_copy.start()

    def send_to(source, target, send, recv, m, own):
        for h in range(2):
            other = 2 * m + sides[h]
            for k in range(1 if own and h == 0 else 0, N_WIN):
                pltpu.make_async_remote_copy(
                    source.at[other * N_WIN + wins[k]], target.at[me], send, recv,
                    device_id=(other, wins[k]), device_id_type=MESH,
                ).start()

    def send_spectra(step, _):
        m = lax.rem(pair + step, PAIRS)
        send_to(sent, got, send_sem, recv_sems.at[pair], m, False)
        return 0

    send_to(sent, got, send_sem, recv_sems.at[pair], pair, True)
    lax.fori_loop(1, PAIRS, send_spectra, 0)

    wanted_all = fold_block[...] * CH_DEV + fold_offset[...]
    fold_offset[...] = wanted_all

    def choose(g, _):
        lanes = pl.ds(pl.multiple_of(g * 256, 256), 256)
        rows = lax.broadcasted_iota(jnp.int32, (CHANNELS, 256), 0)
        chosen[:, lanes] = jnp.where(rows == fold_offset[:, lanes], 1.0, 0.0).astype(BF16)
        return 0

    lax.fori_loop(0, CHANNELS // 256, choose, 0)
    x[:, CHANNELS : CHANNELS + 128] = jnp.zeros((2 * WINDOWS, 128), BF16)

    def all_of(source, target, send, recv, count):
        some = pl.ds(0, count)
        return pltpu.make_async_remote_copy(
            source.at[some], target.at[some], send, recv,
            device_id=neighbour, device_id_type=MESH,
        )

    low_w = lax.broadcasted_iota(jnp.int32, (WINDOWS, 128), 1) < CH_DEV
    low_out = lax.broadcasted_iota(jnp.int32, (128, 128), 1) < CH_DEV
    row_ids = lax.broadcasted_iota(jnp.int32, (128, 128), 0)
    lane_ids = lax.broadcasted_iota(jnp.int32, (128, 128), 1)
    mirror = jnp.where(row_ids + lane_ids == 127, 1.0, 0.0).astype(BF16)
    over_rows = (((0,), (0,)), ((), ()))

    def unpack(m):
        all_of(sent, got, send_sem, recv_sems.at[m], PAIR).wait_recv()
        even = got[pl.ds(PAIR * m, N_WIN)].astype(F32).reshape(WINDOWS, 128)
        odd = got[pl.ds(PAIR * m + N_WIN, N_WIN)].astype(F32).reshape(WINDOWS, 128)
        lanes = pl.ds(pl.multiple_of(m * 128, 128), 128)
        x[0:WINDOWS, lanes] = jnp.where(low_w, even, pltpu.roll(odd, CH_DEV, 1)).astype(BF16)
        x[WINDOWS : 2 * WINDOWS, lanes] = jnp.where(low_w, pltpu.roll(even, CH_DEV, 1), odd).astype(BF16)

    def near(m):
        right = x[:, pl.ds(pl.multiple_of(m * 128, 128), 256)]
        left = jnp.dot(right[:, :128], mirror, preferred_element_type=F32)
        turned = jnp.concatenate([left[WINDOWS:], -left[:WINDOWS]], axis=0).astype(BF16)
        left = left.astype(BF16)
        re = lax.dot_general(left, right, over_rows, preferred_element_type=F32)
        im = lax.dot_general(turned, right, over_rows, preferred_element_type=F32)
        re = pltpu.roll(re, 128, 1, stride=1, stride_axis=0)[:, :128]
        im = pltpu.roll(im, 192, 1, stride=1, stride_axis=0)[:, :128]
        both = jnp.where(low_out, re, im).astype(BF16)
        for g in range(PAIR):
            band[PAIR * m + PAIR - 1 - g] = both[g * ROWS : (g + 1) * ROWS]

    def send_band(m, own):
        send_to(band, band_in, band_send, band_recv, m, own)

    unpack(pair)

    def arrive(step, _):
        m = lax.rem(pair + PAIRS - step, PAIRS)
        unpack(m)
        near(m)
        send_band(m, False)
        return 0

    lax.fori_loop(1, PAIRS - 1, arrive, 0)
    last = lax.rem(pair + 1, PAIRS)
    unpack(last)

    low_1 = lax.broadcasted_iota(jnp.int32, (2, 128), 1) < CH_DEV

    def fold_group(g, _):
        lanes = pl.ds(pl.multiple_of(g * 256, 256), 256)
        partner = jnp.dot(x[:, 0:CHANNELS], chosen[:, lanes], preferred_element_type=F32)
        own = x[:, lanes].astype(F32)
        re_a, im_a = own[:WINDOWS], own[WINDOWS:]
        re_b, im_b = partner[:WINDOWS], partner[WINDOWS:]
        re_c = jnp.sum(re_a * re_b + im_a * im_b, axis=0, keepdims=True)
        im_c = jnp.sum(im_a * re_b - re_a * im_b, axis=0, keepdims=True)
        re_c = jnp.broadcast_to(re_c, (2, 256))
        im_c = jnp.broadcast_to(im_c, (2, 256))
        for half in range(2):
            re_p = re_c[:, half * 128 : half * 128 + 128]
            im_p = im_c[:, half * 128 : half * 128 + 128]
            even = jnp.where(low_1, re_p, pltpu.roll(im_p, CH_DEV, 1)).astype(BF16)
            odd = jnp.where(low_1, pltpu.roll(re_p, CH_DEV, 1), im_p).astype(BF16)
            folded[4 * g + 2 * half] = even
            folded[4 * g + 2 * half + 1] = odd
        return 0

    lax.fori_loop(0, CHANNELS // 256, fold_group, 0)

    own_fold = pltpu.make_async_copy(folded.at[chan], folded_in.at[win, chan], own_sems.at[0])
    own_fold.start()

    def send_fold(step, _):
        other = lax.rem(chan + step, N_CHAN)
        pltpu.make_async_remote_copy(
            folded.at[other], folded_in.at[win, chan], fold_send, fold_recv,
            device_id=(other, win), device_id_type=MESH,
        ).start()
        return 0

    lax.fori_loop(1, N_CHAN, send_fold, 0)

    near(last)
    send_band(last, False)
    near(pair)
    own_band = pltpu.make_async_copy(band.at[me], band_in.at[me], own_sems.at[1])
    own_band.start()
    send_band(pair, True)

    own_fold.wait()
    fold_copies = all_of(folded, folded, fold_send, fold_recv, N_CHAN - 1)
    fold_copies.wait_recv()

    def relay(step, _):
        pltpu.make_async_remote_copy(
            folded_in.at[win], folded_in.at[win], relay_send, relay_recv,
            device_id=(chan, lax.rem(win + step, N_WIN)), device_id_type=MESH,
        ).start()
        return 0

    lax.fori_loop(1, N_WIN, relay, 0)

    all_of(sent, got, send_sem, recv_sems.at[0], DEVICES - 1).wait_send()
    band_copies = all_of(band, band_in, band_send, band_recv, DEVICES - 1)
    band_copies.wait_send()
    band_copies.wait_recv()
    own_band.wait()
    small_copies[4].wait()

    flat[...] = band_in[...].astype(F32).reshape(DEVICES * ROWS, 128)
    for r in range(ROWS):
        turned = flat[pl.ds(r, F, stride=ROWS), :].T
        at = (ROWS - 1 - r) * REACH
        lag_in[0, at : at + REACH, :] = turned[:REACH].astype(BF16)
        lag_in[1, at : at + REACH, :] = turned[REACH:].astype(BF16)
    def transform(first, count):
        total = jnp.zeros((count, NLAG), F32)
        for part in range(2):
            for half in range(2):
                rows = lag_in[part, first : first + count, :]
                total += jnp.dot(rows, inverse[2 * part + half], preferred_element_type=F32)
        return total

    end = ROWS * REACH
    near_ref[...] = transform(0, end).reshape(ROWS, REACH, NLAG)

    fold_copies.wait_send()
    relay_copies = all_of(folded_in, folded_in, relay_send, relay_recv, N_WIN - 1)
    relay_copies.wait_send()
    relay_copies.wait_recv()

    flat_fold[...] = folded_in[...].astype(F32).reshape(DEVICES * 2, 128)
    for w in range(N_WIN):
        rows = flat_fold[pl.ds(2 * N_CHAN * w, N_CHAN, stride=2), :]
        by_bin[pl.ds(w, N_CHAN, stride=N_WIN), :] = rows
    turned_fold[...] = by_bin[...].T
    own = pl.multiple_of(win * ROWS, ROWS)
    pad = jnp.zeros((ROWS, F), F32)
    for part in range(2):
        mine = turned_fold[pl.ds(part * CH_DEV + own, ROWS), :]
        lag_in[part, end : end + 2 * ROWS, :] = jnp.concatenate([mine, pad], axis=0).astype(BF16)
    fold_ref[...] = transform(end, 2 * ROWS)[:ROWS]


def hand_over(near_in, fold_in, near_out, fold_out):
    factor = 1.0 / math.sqrt(F * WINDOWS)
    near_out[...] = near_in[...] * factor
    fold_out[...] = fold_in[...] * factor


def local(traces, quality, fold_block, fold_offset):
    vmem = pl.BlockSpec(memory_space=pltpu.VMEM)
    hbm = pl.BlockSpec(memory_space=pltpu.MemorySpace.HBM)
    phases, inverse = forward_phases(), inverse_halves()
    sem = pltpu.SemaphoreType.DMA
    near_lags, fold_lags = pl.pallas_call(
        kernel,
        out_shape=(
            jax.ShapeDtypeStruct((ROWS, REACH, NLAG), F32),
            jax.ShapeDtypeStruct((ROWS, NLAG), F32),
        ),
        in_specs=[hbm] * 6,
        out_specs=(vmem, vmem),
        scratch_shapes=[
            pltpu.VMEM((CHUNKS, LANES, L), BF16),
            pltpu.VMEM((1, CH_DEV), jnp.int32),
            pltpu.VMEM((1, CHANNELS), jnp.int32),
            pltpu.VMEM((1, CHANNELS), jnp.int32),
            pltpu.VMEM(phases.shape, F32),
            pltpu.VMEM(inverse.shape, BF16),
            pltpu.VMEM((2, F, L), BF16),
            pltpu.VMEM((2, HALF + 16, LANES), F32),
            pltpu.VMEM((F * GROUP, 128), F32),
            pltpu.VMEM((DEVICES, CHUNKS, GROUP, 128), BF16),
            pltpu.VMEM((DEVICES, CHUNKS, GROUP, 128), BF16),
            pltpu.VMEM((2 * WINDOWS, CHANNELS + 128), BF16),
            pltpu.VMEM((CHANNELS, CHANNELS), BF16),
            pltpu.VMEM((DEVICES, ROWS, 128), BF16),
            pltpu.VMEM((N_CHAN, 2, 128), BF16),
            pltpu.VMEM((DEVICES, ROWS, 128), BF16),
            pltpu.VMEM((N_WIN, N_CHAN, 2, 128), BF16),
            pltpu.VMEM((DEVICES * ROWS, 128), F32),
            pltpu.VMEM((DEVICES * 2, 128), F32),
            pltpu.VMEM((F, 128), F32),
            pltpu.VMEM((2, ROWS * REACH + 2 * ROWS, F), BF16),
            pltpu.VMEM((128, F), F32),
            sem((CHUNKS,)),
            sem((5,)),
            sem((2,)),
            sem,
            sem((PAIRS,)),
            sem, sem, sem, sem, sem, sem,
        ],
        compiler_params=pltpu.CompilerParams(
            vmem_limit_bytes=60 << 20, collective_id=0, has_side_effects=True
        ),
    )(
        traces.reshape(WIN_DEV * CH_DEV, L),
        quality.reshape(1, CH_DEV),
        fold_block.reshape(1, CHANNELS),
        fold_offset.reshape(1, CHANNELS),
        phases,
        inverse,
    )
    shapes = tuple(jax.ShapeDtypeStruct(a.shape, a.dtype) for a in (near_lags, fold_lags))
    return pl.pallas_call(
        hand_over,
        grid=(2,),
        out_shape=shapes,
        in_specs=[
            pl.BlockSpec((ROWS // 2, REACH, NLAG), lambda i: (i, 0, 0)),
            pl.BlockSpec((ROWS, NLAG), lambda i: (0, 0)),
        ],
        out_specs=(
            pl.BlockSpec((ROWS // 2, REACH, NLAG), lambda i: (i, 0, 0)),
            pl.BlockSpec((ROWS, NLAG), lambda i: (0, 0)),
        ),
        compiler_params=pltpu.CompilerParams(vmem_limit_bytes=60 << 20),
    )(near_lags, fold_lags)


def solution(mesh):
    in_specs = (P("win", "chan", None), P("chan"), P(), P())
    out_specs = (P(("chan", "win"), None, None), P(("chan", "win"), None))
    return jax.shard_map(local, mesh=mesh, in_specs=in_specs, out_specs=out_specs, check_vma=False)
```
